256 devices in a mesh: inner: 4 (over x_hi, core), outer: 64 (over y, z, x_lo).
Axes of the slice: x: 4 (x_hi: 2, x_lo: 2; x = x_hi * 2 + x_lo), y: 4, z: 8, core: 2. Of those that a mesh axis runs over, the one named last changes fastest.
Arguments:
- q_nope: bfloat16 [16384, 1024], P(('inner', 'outer')), may hold values from -6 to 6
- q_rope: bfloat16 [16384, 512], P(('inner', 'outer')), may hold values from -48 to 48
- kv_compressed: bfloat16 [16384, 576], P(('inner', 'outer')), may hold values from -16 to 16
- token_pos: int32 [16384], P(('inner', 'outer')), may hold values from 0 to 16383, as said below
- kv_gain: float32 [512], replicated, may hold values from 0.25 to 1.75
- w_uk: bfloat16 [8, 128, 512], replicated, may hold values from -0.5 to 0.5
- w_uv: bfloat16 [8, 512, 128], replicated, may hold values from -0.25 to 0.25
Outputs:
- attn_out: bfloat16 [16384, 1024], P(('inner', 'outer'))
The draws below stay inside these ranges and needn't reach their ends.
Inputs may be any that keep to these rules, and one draw needn't show every extreme that they name: `token_pos`: every position 0 to 16383 occurs once; each device's 64 rows are two runs of 32 consecutive increasing positions, span c and span 2 * 256 - 1 - c of the sequence's spans of 32 positions, c differing between devices.
All inputs are finite; a program needn't handle non-finite values.
Results may differ from the reference program's by a relative error of at most 0.012.
The reference program's roundings to bfloat16 on the way (of `latent`, `k_roped`, `q_roped`, `q_absorbed`, `weight` and `o_latent`) count: a program that leaves them out, or rounds other values in their place, can miss the bound.
Values may be sent and summed in bfloat16 or wider, within the bound.
No kernel may reach another device: no remote copies, remote signals or barrier semaphores. Data moves between devices by JAX's collectives and lax.ppermute only.
A program may use at most 192 MiB of HBM per device.

```python
import math
import jax
import jax.numpy as jnp
from jax import lax

D_LATENT = 512
D_ROPE = 64
D_NOPE = 128
D_VALUE = 128
HEADS = 8
TOK_DEV = 64
TOKENS = 16384


def draw_kv_compressed(key, part):
    base = jnp.clip(jax.random.normal(jax.random.fold_in(key, 1), (TOKENS, D_LATENT + D_ROPE), jnp.float32), -6.0, 6.0)
    return base.astype(jnp.bfloat16)


def draw_q_rope(key, part):
    base = jnp.clip(jax.random.normal(jax.random.fold_in(key, 3), (TOKENS, HEADS * D_ROPE), jnp.float32), -6.0, 6.0)
    return base.astype(jnp.bfloat16)


def draw_token_pos(key, part):
    half = TOK_DEV // 2
    devices = TOKENS // TOK_DEV
    order = jax.random.permutation(jax.random.fold_in(key, 5), devices).astype(jnp.int32)
    upper = 2 * devices - 1 - order
    offsets = jnp.arange(half, dtype=jnp.int32)
    low_run = order[:, None] * half + offsets[None, :]
    high_run = upper[:, None] * half + offsets[None, :]
    return jnp.concatenate([low_run, high_run], axis=1).reshape(TOKENS).astype(jnp.int32)


def levels(own_key, extent, cuts, low, largest):
    level, own = 1.0, jax.random.fold_in(own_key, 6)
    for dim, shards_of in cuts:
        steps = jnp.exp(jax.random.uniform(jax.random.fold_in(own, dim), (shards_of,), jnp.float32, low / len(cuts), largest / len(cuts)))
        level = level * jnp.repeat(steps, extent[dim] // shards_of).reshape([-1 if axis == dim else 1 for axis in range(len(extent))])
    return level


def scatter_about(stream_key, extent, spread, reach, cuts=(), kind=jnp.bfloat16):
    factor_of = levels(stream_key, extent, cuts, -0.22, 0.18) if cuts else 1.0
    values = jax.random.normal(stream_key, extent, jnp.float32) * spread * factor_of
    return jnp.minimum(jnp.maximum(values, -reach), reach).astype(kind)


def setup_inputs(seed: int = 0) -> dict:
    splits = jax.random.split(jax.random.key(seed), 8)
    q_nope = scatter_about(splits[0], (TOKENS, HEADS * D_NOPE), 1.0, 6.0, ((0, 256),))
    q_rope = draw_q_rope(jax.random.fold_in(splits[7], 71), 0)
    kv_compressed = draw_kv_compressed(jax.random.fold_in(splits[7], 71), 0)
    token_pos = draw_token_pos(jax.random.fold_in(splits[7], 71), 0)
    kv_gain = jnp.clip(1.0 + 0.15 * jax.random.normal(splits[4], (D_LATENT,), jnp.float32), 0.25, 1.75)
    w_uk = scatter_about(splits[5], (HEADS, D_NOPE, D_LATENT), D_NOPE ** -0.5, 0.5)
    w_uv = scatter_about(splits[6], (HEADS, D_LATENT, D_VALUE), D_LATENT ** -0.5, 0.25)
    return dict(q_nope=q_nope, q_rope=q_rope, kv_compressed=kv_compressed, token_pos=token_pos, kv_gain=kv_gain, w_uk=w_uk, w_uv=w_uv)


def rotate(values, positions):
    half = values.shape[-1] // 2
    freqs = 10000.0 ** (-jnp.arange(half, dtype=jnp.float32) / half)
    angle = positions.astype(jnp.float32)[:, None] * freqs[None, :]
    cosine = jnp.cos(angle)[:, None, :]
    sine = jnp.sin(angle)[:, None, :]
    first = values[..., :half]
    second = values[..., half:]
    return jnp.concatenate([first * cosine - second * sine, second * cosine + first * sine], axis=-1)

def reference(q_nope, q_rope, kv_compressed, token_pos, kv_gain, w_uk, w_uv):
    heads = w_uk.shape[0]
    d_latent = kv_gain.shape[0]
    d_nope = w_uk.shape[1]
    d_rope = kv_compressed.shape[1] - d_latent
    count = q_nope.shape[0]
    comp = kv_compressed.astype(jnp.float32)
    raw_latent = comp[:, :d_latent]
    mean_sq = lax.optimization_barrier(jnp.mean(raw_latent * raw_latent, axis=1, keepdims=True))
    latent = (raw_latent * lax.rsqrt(mean_sq + 1e-06) * kv_gain[None, :]).astype(jnp.bfloat16)
    k_roped = rotate(comp[:, None, d_latent:], token_pos)[:, 0, :].astype(jnp.bfloat16)
    q_roped = rotate(q_rope.astype(jnp.float32).reshape(count, heads, d_rope), token_pos).astype(jnp.bfloat16)
    q_absorbed = jnp.einsum('thd,hde->the', q_nope.astype(jnp.float32).reshape(count, heads, d_nope), w_uk.astype(jnp.float32)).astype(jnp.bfloat16)
    keys = jnp.concatenate([latent, k_roped], axis=1).astype(jnp.float32)
    queries = jnp.concatenate([q_absorbed, q_roped], axis=2)
    scale = 1.0 / math.sqrt(d_nope + d_rope)
    block = math.gcd(count, 512)
    latent_wide = latent.astype(jnp.float32)

    def one_block(index):
        start = (index * block).astype(jnp.int32)
        query_block = lax.dynamic_slice_in_dim(queries, start, block, 0).astype(jnp.float32)
        query_pos = lax.dynamic_slice_in_dim(token_pos, start, block, 0)
        score = jnp.einsum('thd,ud->htu', query_block, keys) * scale
        visible = (token_pos[None, :] <= query_pos[:, None])[None, :, :]
        peak = lax.optimization_barrier(jnp.max(jnp.where(visible, score, -1e+30), axis=2, keepdims=True))
        expd = jnp.where(visible, jnp.exp(score - peak), 0.0)
        total = lax.optimization_barrier(jnp.sum(expd, axis=2))
        weight = expd.astype(jnp.bfloat16).astype(jnp.float32)
        summed = jnp.einsum('htu,ud->htd', weight, latent_wide)
        o_latent = (summed / total[:, :, None]).astype(jnp.bfloat16)
        result = jnp.einsum('htd,hde->the', o_latent.astype(jnp.float32), w_uv.astype(jnp.float32))
        return result.reshape(block, -1).astype(jnp.bfloat16)
    blocks = lax.map(one_block, jnp.arange(count // block, dtype=jnp.int32))
    return blocks.reshape(count, -1)
```

```python
import functools
import math

import jax
import jax.numpy as jnp
import numpy as np
from jax import lax
from jax.experimental import pallas as pl
from jax.experimental.pallas import tpu as pltpu
from jax.sharding import Mesh
from jax.sharding import PartitionSpec as P

ALL_AXES = ("x_hi", "core", "y", "z", "x_lo")
ACROSS = ("x_hi", "x_lo")
X_SIZE, Y_SIZE, Z_SIZE = 4, 4, 8

RUN = 32
TOK = 2 * RUN
D_LAT = 512
HEADS = 8
D_NOPE = 128
D_VAL = 128
ROW = D_LAT + 128
Q_ROW = HEADS * D_NOPE + 512 + 128
OUT_ROW = HEADS * D_VAL + 128
Q_TILE = 2 * X_SIZE * RUN
SPANS = 512

NEGATIVE = -1e30
FLOOR = -1e28
LOG2E = 1.4426950408889634

VMEM = pl.BlockSpec(memory_space=pltpu.VMEM)
SMEM = pl.BlockSpec(memory_space=pltpu.SMEM)


def lanes(rows):
    return lax.broadcasted_iota(jnp.int32, (rows, 128), 1)


def turned(values, cosine, sine, first):
    partner = jnp.where(first, pltpu.roll(values, 96, 1), pltpu.roll(values, 32, 1))
    return values * cosine + partner * jnp.where(first, -sine, sine)


def rows_kernel(pos_ref, low_ref, high_ref, step_ref, qn_ref, qr_ref, kv_ref, gain_ref, key_ref, q_ref):
    lane = lanes(RUN)
    first = lane % 64 < 32
    slot = lax.axis_index("y") * Z_SIZE + lax.axis_index("z")
    turn = jnp.where(pos_ref[0] < pos_ref[RUN], 0, RUN)
    span = (jnp.minimum(pos_ref[0], pos_ref[RUN]) // RUN + 1).astype(jnp.float32)
    step_cos, step_sin = step_ref[0], step_ref[1]
    for half, base_ref in enumerate((low_ref, high_ref)):
        src = pl.ds(pl.multiple_of(turn if half == 0 else RUN - turn, RUN), RUN)
        dst = slice(half * RUN, (half + 1) * RUN)
        base_cos, base_sin = base_ref[0, 0:1], base_ref[0, 1:2]
        cosine = base_cos * step_cos - base_sin * step_sin
        sine = base_sin * step_cos + base_cos * step_sin

        raw = kv_ref[src, :D_LAT].astype(jnp.float32)
        mean_sq = jnp.mean(raw * raw, axis=1, keepdims=True)
        latent = raw * lax.rsqrt(mean_sq + 1e-06) * gain_ref[...]
        key_ref[dst, :D_LAT] = latent.astype(jnp.bfloat16)
        rope = kv_ref[src, D_LAT:].astype(jnp.float32)
        rope = turned(jnp.concatenate([rope, jnp.zeros_like(rope)], axis=1), cosine, sine, first)
        tail = jnp.where(lane == 64 + slot, span, 0.0)
        key_ref[dst, D_LAT:] = jnp.where(lane < 64, rope, tail).astype(jnp.bfloat16)

        q_ref[dst, : HEADS * D_NOPE] = qn_ref[src, :]
        for pair in range(HEADS // 2):
            part = qr_ref[src, pair * 128 : (pair + 1) * 128].astype(jnp.float32)
            at = HEADS * D_NOPE + pair * 128
            q_ref[dst, at : at + 128] = turned(part, cosine, sine, first).astype(jnp.bfloat16)
        q_ref[dst, Q_ROW - 128 :] = jnp.full((RUN, 128), span, jnp.float32).astype(jnp.bfloat16)


def rotations():
    freqs = np.tile(10000.0 ** (-np.arange(32) / 32.0), 4)
    table = lambda p: np.stack([np.cos(p[:, None] * freqs), np.sin(p[:, None] * freqs)], axis=1)
    spans = table(np.arange(SPANS) * float(RUN)).astype(np.float32)
    steps = table(np.arange(RUN) * 1.0).astype(np.float32).transpose(1, 0, 2)
    return spans, steps


def over_lanes(a, b):
    return lax.dot_general(a, b, (((1,), (1,)), ((), ())), preferred_element_type=jnp.float32)


def expand_kernel(n_keys, *refs):
    key_refs, (uk_ref, uv_ref, k_ref, v_ref, tail_ref) = refs[:n_keys], refs[n_keys:]
    for half in range(2):
        run = slice(half * RUN, (half + 1) * RUN)
        rows = [ref[:, run, :].reshape(-1, ROW) for ref in key_refs]
        rows = jnp.concatenate(rows, axis=0) if n_keys > 1 else rows[0]
        latent = rows[:, :D_LAT]
        tail_ref[half] = rows[:, D_LAT:]
        for pair in range(HEADS // 2):
            cols = slice(pair * 256, (pair + 1) * 256)
            k_ref[half, :, cols] = over_lanes(latent, uk_ref[cols, :]).astype(jnp.bfloat16)
            w = jnp.concatenate([uv_ref[2 * pair], uv_ref[2 * pair + 1]], axis=1)
            v_ref[half, :, cols] = jnp.dot(latent, w, preferred_element_type=jnp.float32).astype(jnp.bfloat16)


def expand(blocks, w_uk, w_uv):
    n = sum(b.shape[0] for b in blocks) * RUN
    out = lambda width: jax.ShapeDtypeStruct((2, n, width), jnp.bfloat16)
    return pl.pallas_call(
        functools.partial(expand_kernel, len(blocks)),
        in_specs=[VMEM] * (len(blocks) + 2),
        out_specs=[VMEM] * 3,
        out_shape=[out(HEADS * D_NOPE), out(HEADS * D_VAL), out(128)],
        compiler_params=pltpu.CompilerParams(vmem_limit_bytes=24 << 20),
        cost_estimate=pl.CostEstimate(
            flops=4 * n * D_LAT * 2048, bytes_accessed=n * 12000 + (2 << 20), transcendentals=0
        ),
        name="expand",
    )(*blocks, w_uk.reshape(HEADS * D_NOPE, D_LAT), w_uv)


def packed(stats):
    top = stats.astype(jnp.bfloat16)
    rest = stats - top.astype(jnp.float32)
    mid = rest.astype(jnp.bfloat16)
    rest = rest - mid.astype(jnp.float32)
    pieces = top.astype(jnp.float32) + pltpu.roll(mid.astype(jnp.float32), 8, 1)
    return (pieces + pltpu.roll(rest, 16, 1)).astype(jnp.bfloat16)


def unpacked(pieces):
    pieces = pieces.astype(jnp.float32)
    return pieces + pltpu.roll(pieces, 120, 1) + pltpu.roll(pieces, 112, 1)


def attend_kernel(n_chunks, scale, *refs):
    near_ref, far_ref = refs[:2]
    k_refs, v_refs, tail_refs = (refs[2 + i * n_chunks : 2 + (i + 1) * n_chunks] for i in range(3))
    outs, lse_scr = refs[2 + 3 * n_chunks : -1], refs[-1]
    step = pl.program_id(0)
    lane = lanes(RUN)
    q_refs = [(ref, i) for ref in (near_ref, far_ref) for i in range(X_SIZE)]
    q_at = pl.multiple_of(step * 256, 256)
    rope_at = pl.multiple_of(HEADS * D_NOPE + step * 128, 128)
    tails = [jnp.concatenate([ref[half] for ref in tail_refs], axis=0) for half in range(2)]
    spans = jnp.max(tails[0].astype(jnp.float32), axis=0, keepdims=True)
    first_keys = tail_refs[0].shape[1]
    shape = (Q_TILE, first_keys)
    row, col = (lax.broadcasted_iota(jnp.int32, shape, d) for d in (0, 1))
    later = (row < RUN) & (col < RUN) & (col > row)

    @pl.when(step == 0)
    def _():
        lse_scr[...] = jnp.zeros_like(lse_scr)

    for half in range(2):
        run = slice(half * RUN, (half + 1) * RUN)
        nope = jnp.concatenate([ref[i, run, pl.ds(q_at, 256)] for ref, i in q_refs], axis=0)
        ropes = [ref[i, run, pl.ds(rope_at, 128)].astype(jnp.float32) for ref, i in q_refs]
        biases = []
        for ref, i in q_refs:
            mine = ref[i, 0:16, Q_ROW - 128 :].astype(jnp.float32)[0:1]
            seen = (spans >= mine) if half else (spans <= mine)
            biases.append(jnp.where(seen, 0.0, NEGATIVE))
        for inner in range(2):
            cols = slice(inner * 128, (inner + 1) * 128)
            turned_by = [pltpu.roll(r, 64, 1) if inner else r for r in ropes]
            ends = lambda fill: jnp.concatenate(
                [jnp.where(lane < 64, r, f) for r, f in zip(turned_by, fill)], axis=0
            ).astype(jnp.bfloat16)
            masked = jnp.concatenate([nope[:, cols], ends(biases)], axis=1)
            keys = lambda run: jnp.concatenate(
                [jnp.concatenate([ref[run, :, cols] for ref in k_refs], axis=0), tails[run]], axis=1
            )
            values = lambda run: jnp.concatenate([ref[run, :, cols] for ref in v_refs], axis=0)
            score = over_lanes(masked, keys(half)) * scale
            head = jnp.where(later, NEGATIVE, score[:, :first_keys])
            parts = [(jnp.concatenate([head, score[:, first_keys:]], axis=1), half)]
            if half:
                plain = jnp.concatenate([nope[:, cols], ends([0.0] * len(q_refs))], axis=1)
                parts.append((over_lanes(plain, keys(0)) * scale, 0))
            peak = functools.reduce(jnp.maximum, [jnp.max(s, axis=1, keepdims=True) for s, _ in parts])
            peak = jnp.maximum(peak, FLOOR)
            total, added = None, None
            for s, run_of in parts:
                expd = jnp.exp2(s - peak)
                t = jnp.sum(expd, axis=1, keepdims=True)
                a = jnp.dot(expd.astype(jnp.bfloat16), values(run_of), preferred_element_type=jnp.float32)
                total = t if total is None else total + t
                added = a if added is None else added + a
            some = total > 0.0
            total = jnp.where(some, total, 1.0)
            result = (added / total).astype(jnp.bfloat16)
            lse = jnp.where(some, peak + jnp.log2(total), NEGATIVE)
            head_at = pl.multiple_of(step * 256 + inner * 128, 128)
            for i in range(2 * X_SIZE):
                rows = slice(i * RUN, (i + 1) * RUN)
                outs[i // X_SIZE][i % X_SIZE, run, pl.ds(head_at, 128)] = result[rows]
                lse_scr[i, run, :] = jnp.where(lane == 2 * step + inner, lse[rows], lse_scr[i, run, :])

    @pl.when(step == HEADS // 2 - 1)
    def _():
        for i in range(2 * X_SIZE):
            outs[i // X_SIZE][i % X_SIZE, :, HEADS * D_VAL :] = packed(lse_scr[i])


def attend(near, far, chunks, scale):
    whole = lambda shape: pl.BlockSpec(shape, lambda i: (0,) * len(shape))
    by_head = lambda a: pl.BlockSpec((2, a.shape[1], 256), lambda i: (0, 0, i))
    ks, vs, tails = zip(*chunks)
    out = jax.ShapeDtypeStruct((X_SIZE, TOK, OUT_ROW), jnp.bfloat16)
    return pl.pallas_call(
        functools.partial(attend_kernel, len(chunks), scale),
        grid=(HEADS // 2,),
        in_specs=[whole(near.shape), whole(far.shape)]
        + [by_head(a) for a in ks + vs]
        + [whole(a.shape) for a in tails],
        out_specs=[whole(out.shape)] * 2,
        out_shape=[out, out],
        scratch_shapes=[pltpu.VMEM((2 * X_SIZE, TOK, 128), jnp.float32)],
        compiler_params=pltpu.CompilerParams(vmem_limit_bytes=48 << 20),
        cost_estimate=pl.CostEstimate(flops=10**10, bytes_accessed=12 << 20, transcendentals=6 * 10**6),
        name="attend",
    )(near, far, *ks, *vs, *tails)


def mix(parts, shares, run, h):
    cols = slice(h * D_VAL, (h + 1) * D_VAL)
    terms = [p[run, cols].astype(jnp.float32) * s[run, h : h + 1] for p, s in zip(parts, shares)]
    return functools.reduce(jnp.add, terms)


def merge_kernel(near_ref, far_ref, *out_refs):
    for i, out_ref in enumerate(out_refs, 1):
        parts = [near_ref.at[i], far_ref.at[i]]
        stats = [unpacked(p[:, HEADS * D_VAL :]) for p in parts]
        best = functools.reduce(jnp.maximum, stats)
        shares = [jnp.exp2(s - best) for s in stats]
        whole = functools.reduce(jnp.add, shares)
        used = lanes(TOK) < HEADS
        out_ref[:, HEADS * D_VAL :] = packed(jnp.where(used, best + jnp.log2(whole), 0.0))
        shares = [s / whole for s in shares]
        for h in range(HEADS):
            out_ref[:, h * D_VAL : (h + 1) * D_VAL] = mix(parts, shares, slice(0, TOK), h).astype(jnp.bfloat16)


def combine_kernel(pos_ref, near_ref, far_ref, *refs):
    parts, out_ref = [near_ref.at[0], far_ref.at[0], *refs[:-1]], refs[-1]
    stats = [unpacked(p[:, HEADS * D_VAL :]) for p in parts]
    best = functools.reduce(jnp.maximum, stats)
    shares = [jnp.exp2(s - best) for s in stats]
    whole = functools.reduce(jnp.add, shares)
    shares = [s / whole for s in shares]
    turn = jnp.where(pos_ref[0] < pos_ref[RUN], 0, RUN)
    for half in range(2):
        dst = pl.ds(pl.multiple_of(turn if half == 0 else RUN - turn, RUN), RUN)
        run = slice(half * RUN, (half + 1) * RUN)
        for h in range(HEADS):
            out_ref[dst, h * D_VAL : (h + 1) * D_VAL] = mix(parts, shares, run, h).astype(jnp.bfloat16)


def shift(size, by):
    return [(i, (i + by) % size) for i in range(size)]


def body(q_nope, q_rope, kv_compressed, token_pos, kv_gain, w_uk, w_uv):
    scale = LOG2E / math.sqrt(D_NOPE + 64)
    spans, steps = rotations()
    low_span = lambda i, pos: (jnp.minimum(pos[0], pos[RUN]) // RUN, 0, 0)
    high_span = lambda i, pos: (jnp.maximum(pos[0], pos[RUN]) // RUN, 0, 0)
    whole = lambda shape: pl.BlockSpec(shape, lambda i, pos: (0,) * len(shape))
    key_rows, q_rows = pl.pallas_call(
        rows_kernel,
        grid_spec=pltpu.PrefetchScalarGridSpec(
            num_scalar_prefetch=1,
            grid=(1,),
            in_specs=[
                pl.BlockSpec((1, 2, 128), low_span),
                pl.BlockSpec((1, 2, 128), high_span),
                whole((2, RUN, 128)),
                whole(q_nope.shape),
                whole(q_rope.shape),
                whole(kv_compressed.shape),
                whole((1, D_LAT)),
            ],
            out_specs=[whole((TOK, ROW)), whole((TOK, Q_ROW))],
        ),
        out_shape=[
            jax.ShapeDtypeStruct((TOK, ROW), jnp.bfloat16),
            jax.ShapeDtypeStruct((TOK, Q_ROW), jnp.bfloat16),
        ],
        name="rows",
    )(token_pos, spans, spans, steps, q_nope, q_rope, kv_compressed, kv_gain[None, :])

    swap = lambda block: lax.ppermute(block, "core", [(0, 1), (1, 0)])
    across = lambda block, by: lax.ppermute(block, ACROSS, shift(X_SIZE, by))
    along = lambda block, by: lax.ppermute(block, "z", shift(Z_SIZE, by))

    along_y = [key_rows] + [lax.ppermute(key_rows, "y", shift(Y_SIZE, by)) for by in (1, -1, 2)]
    mine = jnp.stack(along_y)
    mine, q_rows = lax.optimization_barrier((mine, q_rows))

    up, down = along(mine, 1), along(mine, -1)
    near = jnp.stack([q_rows] + [across(q_rows, by) for by in (1, -1, 2)])
    far = swap(near)
    chunks = [expand([mine], w_uk, w_uv)]
    up, down, near, chunks = lax.optimization_barrier((up, down, near, chunks))
    for hop in range(2, Z_SIZE // 2 + 1):
        blocks = [up, down]
        if hop == Z_SIZE // 2:
            up, down = up[: Y_SIZE // 2], down[Y_SIZE // 2 :]
        up, down = along(up, 1), along(down, -1)
        chunks.append(expand(blocks, w_uk, w_uv))
        up, down, chunks = lax.optimization_barrier((up, down, chunks))
    chunks.append(expand([up, down], w_uk, w_uv))

    near, far = attend(near, far, chunks, scale)
    far = swap(far)
    part = jax.ShapeDtypeStruct((TOK, OUT_ROW), jnp.bfloat16)
    merged = pl.pallas_call(
        merge_kernel,
        in_specs=[VMEM] * 2,
        out_specs=[VMEM] * 3,
        out_shape=[part] * 3,
        name="merge",
    )(near, far)
    back = [across(m, by) for m, by in zip(merged, (-1, 1, 2))]
    return pl.pallas_call(
        combine_kernel,
        in_specs=[SMEM] + [VMEM] * 5,
        out_specs=VMEM,
        out_shape=jax.ShapeDtypeStruct((TOK, HEADS * D_VAL), jnp.bfloat16),
        name="combine",
    )(token_pos, near, far, *back)


def solution(mesh):
    finer = Mesh(mesh.devices.reshape(2, 2, Y_SIZE, Z_SIZE, 2), ALL_AXES)
    rows = P(ALL_AXES, None)
    in_specs = (rows, rows, rows, P(ALL_AXES), P(), P(), P())
    return jax.shard_map(body, mesh=finer, in_specs=in_specs, out_specs=rows, check_vma=False)
```

```python
import functools
import math

import jax
import jax.numpy as jnp
import numpy as np
from jax import lax
from jax.experimental import pallas as pl
from jax.experimental.pallas import tpu as pltpu
from jax.sharding import Mesh
from jax.sharding import PartitionSpec as P

ALL_AXES = ("x_hi", "core", "y", "z", "x_lo")
ACROSS = ("x_hi", "x_lo")
X_SIZE, Y_SIZE, Z_SIZE = 4, 4, 8

RUN = 32
TOK = 2 * RUN
D_LAT = 512
HEADS = 8
D_NOPE = 128
D_VAL = 128
ROW = D_LAT + 128
Q_ROW = HEADS * D_NOPE + 512 + 128
OUT_ROW = HEADS * D_VAL + 128
Q_TILE = 2 * X_SIZE * RUN
SPANS = 512

NEGATIVE = -1e30
FLOOR = -1e28
SCALE = 1.4426950408889634 / math.sqrt(D_NOPE + 64)

VMEM = pl.BlockSpec(memory_space=pltpu.VMEM)
SMEM = pl.BlockSpec(memory_space=pltpu.SMEM)


def lanes(rows):
    return lax.broadcasted_iota(jnp.int32, (rows, 128), 1)


def turned(values, cosine, sine, first):
    partner = jnp.where(first, pltpu.roll(values, 96, 1), pltpu.roll(values, 32, 1))
    return values * cosine + partner * jnp.where(first, -sine, sine)


def rows_kernel(pos_ref, low_ref, high_ref, step_ref, qn_ref, qr_ref, kv_ref, gain_ref, key_ref, q_ref):
    lane = lanes(RUN)
    first = lane % 64 < 32
    slot = lax.axis_index("y") * Z_SIZE + lax.axis_index("z")
    turn = jnp.where(pos_ref[0] < pos_ref[RUN], 0, RUN)
    span = (jnp.minimum(pos_ref[0], pos_ref[RUN]) // RUN + 1).astype(jnp.float32)
    step_cos, step_sin = step_ref[0], step_ref[1]
    for half, base_ref in enumerate((low_ref, high_ref)):
        src = pl.ds(pl.multiple_of(turn if half == 0 else RUN - turn, RUN), RUN)
        dst = slice(half * RUN, (half + 1) * RUN)
        base_cos, base_sin = base_ref[0, 0:1], base_ref[0, 1:2]
        cosine = base_cos * step_cos - base_sin * step_sin
        sine = base_sin * step_cos + base_cos * step_sin

        raw = kv_ref[src, :D_LAT].astype(jnp.float32)
        mean_sq = jnp.mean(raw * raw, axis=1, keepdims=True)
        latent = raw * lax.rsqrt(mean_sq + 1e-06) * gain_ref[...]
        key_ref[dst, :D_LAT] = latent.astype(jnp.bfloat16)
        rope = kv_ref[src, D_LAT:].astype(jnp.float32)
        rope = turned(jnp.concatenate([rope, jnp.zeros_like(rope)], axis=1), cosine, sine, first)
        tail = jnp.where(lane == 64 + slot, span, 0.0)
        key_ref[dst, D_LAT:] = jnp.where(lane < 64, rope, tail).astype(jnp.bfloat16)

        q_ref[dst, : HEADS * D_NOPE] = qn_ref[src, :]
        for pair in range(HEADS // 2):
            part = qr_ref[src, pair * 128 : (pair + 1) * 128].astype(jnp.float32)
            at = HEADS * D_NOPE + pair * 128
            q_ref[dst, at : at + 128] = (turned(part, cosine, sine, first) * SCALE).astype(jnp.bfloat16)
        q_ref[dst, Q_ROW - 128 :] = jnp.full((RUN, 128), span, jnp.float32).astype(jnp.bfloat16)


def rotations():
    freqs = np.tile(10000.0 ** (-np.arange(32) / 32.0), 4)
    table = lambda p: np.stack([np.cos(p[:, None] * freqs), np.sin(p[:, None] * freqs)], axis=1)
    spans = table(np.arange(SPANS) * float(RUN)).astype(np.float32)
    steps = table(np.arange(RUN) * 1.0).astype(np.float32).transpose(1, 0, 2)
    return spans, steps


def over_lanes(a, b):
    return lax.dot_general(a, b, (((1,), (1,)), ((), ())), preferred_element_type=jnp.float32)


def expand_kernel(n_keys, *refs):
    key_refs, (uk_ref, uv_ref, k_ref, v_ref, tail_ref) = refs[:n_keys], refs[n_keys:]
    for half in range(2):
        run = slice(half * RUN, (half + 1) * RUN)
        rows = [ref[:, run, :].reshape(-1, ROW) for ref in key_refs]
        rows = jnp.concatenate(rows, axis=0) if n_keys > 1 else rows[0]
        latent = rows[:, :D_LAT]
        tail_ref[half] = rows[:, D_LAT:]
        for pair in range(HEADS // 2):
            cols = slice(pair * 256, (pair + 1) * 256)
            k_ref[half, :, cols] = (over_lanes(latent, uk_ref[cols, :]) * SCALE).astype(jnp.bfloat16)
            w = jnp.concatenate([uv_ref[2 * pair], uv_ref[2 * pair + 1]], axis=1)
            v_ref[half, :, cols] = jnp.dot(latent, w, preferred_element_type=jnp.float32).astype(jnp.bfloat16)


def expand(blocks, w_uk, w_uv):
    n = sum(b.shape[0] for b in blocks) * RUN
    out = lambda width: jax.ShapeDtypeStruct((2, n, width), jnp.bfloat16)
    return pl.pallas_call(
        functools.partial(expand_kernel, len(blocks)),
        in_specs=[VMEM] * (len(blocks) + 2),
        out_specs=[VMEM] * 3,
        out_shape=[out(HEADS * D_NOPE), out(HEADS * D_VAL), out(128)],
        compiler_params=pltpu.CompilerParams(vmem_limit_bytes=14 << 20),
        cost_estimate=pl.CostEstimate(
            flops=4 * n * D_LAT * 2048, bytes_accessed=n * 12000 + (2 << 20), transcendentals=0
        ),
        name="expand",
    )(*blocks, w_uk.reshape(HEADS * D_NOPE, D_LAT), w_uv)


def packed(stats):
    top = stats.astype(jnp.bfloat16)
    rest = stats - top.astype(jnp.float32)
    mid = rest.astype(jnp.bfloat16)
    rest = rest - mid.astype(jnp.float32)
    pieces = top.astype(jnp.float32) + pltpu.roll(mid.astype(jnp.float32), 8, 1)
    return (pieces + pltpu.roll(rest, 16, 1)).astype(jnp.bfloat16)


def unpacked(pieces):
    pieces = pieces.astype(jnp.float32)
    return pieces + pltpu.roll(pieces, 120, 1) + pltpu.roll(pieces, 112, 1)


def attend_kernel(n_chunks, own, *refs):
    near_ref, far_ref = refs[:2]
    k_refs, v_refs, tail_refs = (refs[2 + i * n_chunks : 2 + (i + 1) * n_chunks] for i in range(3))
    outs, lse_scr = refs[2 + 3 * n_chunks : -1], refs[-1]
    step = pl.program_id(0)
    lane = lanes(RUN)
    q_refs = [(ref, i) for ref in (near_ref, far_ref) for i in range(X_SIZE)]
    q_at = pl.multiple_of(step * 256, 256)
    rope_at = pl.multiple_of(HEADS * D_NOPE + step * 128, 128)
    tails = [jnp.concatenate([ref[half] for ref in tail_refs], axis=0) for half in range(2)]
    spans = jnp.max(tails[0].astype(jnp.float32), axis=0, keepdims=True)
    ones = jnp.ones((tails[0].shape[0], 128), jnp.bfloat16)
    first_keys = tail_refs[0].shape[1]
    shape = (Q_TILE, first_keys)
    row, col = (lax.broadcasted_iota(jnp.int32, shape, d) for d in (0, 1))
    later = (row < RUN) & (col < RUN) & (col > row)

    @pl.when(step == 0)
    def _():
        lse_scr[...] = jnp.zeros_like(lse_scr)

    for half in range(2):
        run = slice(half * RUN, (half + 1) * RUN)
        nope = jnp.concatenate([ref[i, run, pl.ds(q_at, 256)] for ref, i in q_refs], axis=0)
        ropes = [ref[i, run, pl.ds(rope_at, 128)].astype(jnp.float32) for ref, i in q_refs]
        biases = []
        for ref, i in q_refs:
            mine = ref[i, 0:16, Q_ROW - 128 :].astype(jnp.float32)[0:1]
            seen = (spans >= mine) if half else (spans <= mine)
            biases.append(jnp.where(seen, 0.0, NEGATIVE))
        for inner in range(2):
            cols = slice(inner * 128, (inner + 1) * 128)
            turned_by = [pltpu.roll(r, 64, 1) if inner else r for r in ropes]
            ends = lambda fill: jnp.concatenate(
                [jnp.where(lane < 64, r, f) for r, f in zip(turned_by, fill)], axis=0
            ).astype(jnp.bfloat16)
            masked = jnp.concatenate([nope[:, cols], ends(biases)], axis=1)
            keys = lambda run: jnp.concatenate(
                [jnp.concatenate([ref[run, :, cols] for ref in k_refs], axis=0), tails[run]], axis=1
            )
            values = lambda run: jnp.concatenate(
                [jnp.concatenate([ref[run, :, cols] for ref in v_refs], axis=0), ones], axis=1
            )
            score = over_lanes(masked, keys(half))
            if own:
                head = jnp.where(later, NEGATIVE, score[:, :first_keys])
                score = jnp.concatenate([head, score[:, first_keys:]], axis=1)
            parts = [(score, half)]
            if half:
                plain = jnp.concatenate([nope[:, cols], ends([0.0] * len(q_refs))], axis=1)
                parts.append((over_lanes(plain, keys(0)), 0))
            peak = functools.reduce(jnp.maximum, [jnp.max(s, axis=1, keepdims=True) for s, _ in parts])
            peak = jnp.maximum(peak, FLOOR)
            added = None
            for s, run_of in parts:
                weight = jnp.exp2(s - peak).astype(jnp.bfloat16)
                a = jnp.dot(weight, values(run_of), preferred_element_type=jnp.float32)
                added = a if added is None else added + a
            some = added[:, D_VAL:] > 0.0
            total = jnp.where(some, added[:, D_VAL:], 1.0)
            result = (added[:, :D_VAL] / total).astype(jnp.bfloat16)
            lse = jnp.where(some, peak + jnp.log2(total), NEGATIVE)
            head_at = pl.multiple_of(step * 256 + inner * 128, 128)
            for i in range(2 * X_SIZE):
                rows = slice(i * RUN, (i + 1) * RUN)
                outs[i // X_SIZE][i % X_SIZE, run, pl.ds(head_at, 128)] = result[rows]
                lse_scr[i, run, :] = jnp.where(lane == 2 * step + inner, lse[rows], lse_scr[i, run, :])

    @pl.when(step == HEADS // 2 - 1)
    def _():
        for i in range(2 * X_SIZE):
            outs[i // X_SIZE][i % X_SIZE, :, HEADS * D_VAL :] = packed(lse_scr[i])


def attend(near, far, chunks, own):
    whole = lambda shape: pl.BlockSpec(shape, lambda i: (0,) * len(shape))
    by_head = lambda a: pl.BlockSpec((2, a.shape[1], 256), lambda i: (0, 0, i))
    ks, vs, tails = zip(*chunks)
    out = jax.ShapeDtypeStruct((X_SIZE, TOK, OUT_ROW), jnp.bfloat16)
    return pl.pallas_call(
        functools.partial(attend_kernel, len(chunks), own),
        grid=(HEADS // 2,),
        in_specs=[whole(near.shape), whole(far.shape)]
        + [by_head(a) for a in ks + vs]
        + [whole(a.shape) for a in tails],
        out_specs=[whole(out.shape)] * 2,
        out_shape=[out, out],
        scratch_shapes=[pltpu.VMEM((2 * X_SIZE, TOK, 128), jnp.float32)],
        compiler_params=pltpu.CompilerParams(vmem_limit_bytes=22 << 20),
        cost_estimate=pl.CostEstimate(
            flops=10**7 * sum(a.shape[1] for a in ks), bytes_accessed=8 << 20, transcendentals=3 * 10**6
        ),
        name="attend",
    )(near, far, *ks, *vs, *tails)


def mix(parts, shares, run, h):
    cols = slice(h * D_VAL, (h + 1) * D_VAL)
    terms = [p[run, cols].astype(jnp.float32) * s[run, h : h + 1] for p, s in zip(parts, shares)]
    return functools.reduce(jnp.add, terms)


def merge_kernel(n_parts, *refs):
    for i, out_ref in enumerate(refs[n_parts:], 1):
        parts = [ref.at[i] for ref in refs[:n_parts]]
        stats = [unpacked(p[:, HEADS * D_VAL :]) for p in parts]
        best = functools.reduce(jnp.maximum, stats)
        shares = [jnp.exp2(s - best) for s in stats]
        whole = functools.reduce(jnp.add, shares)
        used = lanes(TOK) < HEADS
        out_ref[:, HEADS * D_VAL :] = packed(jnp.where(used, best + jnp.log2(whole), 0.0))
        shares = [s / whole for s in shares]
        for h in range(HEADS):
            out_ref[:, h * D_VAL : (h + 1) * D_VAL] = mix(parts, shares, slice(0, TOK), h).astype(jnp.bfloat16)


def combine_kernel(n_local, pos_ref, *refs):
    parts, out_ref = [ref.at[0] for ref in refs[:n_local]] + list(refs[n_local:-1]), refs[-1]
    stats = [unpacked(p[:, HEADS * D_VAL :]) for p in parts]
    best = functools.reduce(jnp.maximum, stats)
    shares = [jnp.exp2(s - best) for s in stats]
    whole = functools.reduce(jnp.add, shares)
    shares = [s / whole for s in shares]
    turn = jnp.where(pos_ref[0] < pos_ref[RUN], 0, RUN)
    for half in range(2):
        dst = pl.ds(pl.multiple_of(turn if half == 0 else RUN - turn, RUN), RUN)
        run = slice(half * RUN, (half + 1) * RUN)
        for h in range(HEADS):
            out_ref[dst, h * D_VAL : (h + 1) * D_VAL] = mix(parts, shares, run, h).astype(jnp.bfloat16)


def shift(size, by):
    return [(i, (i + by) % size) for i in range(size)]


def body(q_nope, q_rope, kv_compressed, token_pos, kv_gain, w_uk, w_uv):
    spans, steps = rotations()
    low_span = lambda i, pos: (jnp.minimum(pos[0], pos[RUN]) // RUN, 0, 0)
    high_span = lambda i, pos: (jnp.maximum(pos[0], pos[RUN]) // RUN, 0, 0)
    whole = lambda shape: pl.BlockSpec(shape, lambda i, pos: (0,) * len(shape))
    key_rows, q_rows = pl.pallas_call(
        rows_kernel,
        grid_spec=pltpu.PrefetchScalarGridSpec(
            num_scalar_prefetch=1,
            grid=(1,),
            in_specs=[
                pl.BlockSpec((1, 2, 128), low_span),
                pl.BlockSpec((1, 2, 128), high_span),
                whole((2, RUN, 128)),
                whole(q_nope.shape),
                whole(q_rope.shape),
                whole(kv_compressed.shape),
                whole((1, D_LAT)),
            ],
            out_specs=[whole((TOK, ROW)), whole((TOK, Q_ROW))],
        ),
        out_shape=[
            jax.ShapeDtypeStruct((TOK, ROW), jnp.bfloat16),
            jax.ShapeDtypeStruct((TOK, Q_ROW), jnp.bfloat16),
        ],
        name="rows",
    )(token_pos, spans, spans, steps, q_nope, q_rope, kv_compressed, kv_gain[None, :])

    swap = lambda block: lax.ppermute(block, "core", [(0, 1), (1, 0)])
    across = lambda block, by: lax.ppermute(block, ACROSS, shift(X_SIZE, by))
    along = lambda block, by: lax.ppermute(block, "z", shift(Z_SIZE, by))

    along_y = [lax.ppermute(key_rows, "y", shift(Y_SIZE, by)) for by in (1, -1, 2)]
    mine = jnp.stack([key_rows] + along_y)
    from_left = across(q_rows, 1)
    mine, q_rows, from_left = lax.optimization_barrier((mine, q_rows, from_left))

    up, down = along(mine, 1), along(mine, -1)
    opposite = across(q_rows, 2)
    first = [expand([mine], w_uk, w_uv)]
    up, down, opposite, q_rows, first = lax.optimization_barrier((up, down, opposite, q_rows, first))

    blocks = [up, down]
    up, down = along(up, 1), along(down, -1)
    from_right = across(q_rows, -1)
    first.append(expand(blocks, w_uk, w_uv))
    up, down, from_right, first = lax.optimization_barrier((up, down, from_right, first))

    blocks = [up, down]
    up, down = along(up, 1), along(down, -1)
    near = jnp.stack([q_rows, from_left, from_right, opposite])
    far = swap(near)
    second = [expand(blocks, w_uk, w_uv)]
    partials = [attend(near, far, first, True)]
    up, down, second, partials = lax.optimization_barrier((up, down, second, partials))

    blocks = [up, down]
    half = Y_SIZE // 2
    up, down = along(up[:half], 1), along(down[half:], -1)
    crossed = [swap(partials[0][1])]
    third = [expand(blocks, w_uk, w_uv)]
    partials.append(attend(near, far, second, False))
    up, down, third, partials, crossed = lax.optimization_barrier((up, down, third, partials, crossed))

    third.append(expand([up, down], w_uk, w_uv))
    crossed.append(swap(partials[1][1]))
    partials.append(attend(near, far, third, False))
    crossed.append(swap(partials[2][1]))

    local = [p[0] for p in partials] + crossed
    part = jax.ShapeDtypeStruct((TOK, OUT_ROW), jnp.bfloat16)
    merged = pl.pallas_call(
        functools.partial(merge_kernel, len(local)),
        in_specs=[VMEM] * len(local),
        out_specs=[VMEM] * 3,
        out_shape=[part] * 3,
        compiler_params=pltpu.CompilerParams(vmem_limit_bytes=8 << 20),
        name="merge",
    )(*local)
    back = [across(m, by) for m, by in zip(merged, (-1, 1, 2))]
    return pl.pallas_call(
        functools.partial(combine_kernel, len(local)),
        in_specs=[SMEM] + [VMEM] * (len(local) + 3),
        out_specs=VMEM,
        out_shape=jax.ShapeDtypeStruct((TOK, HEADS * D_VAL), jnp.bfloat16),
        compiler_params=pltpu.CompilerParams(vmem_limit_bytes=8 << 20),
        name="combine",
    )(token_pos, *local, *back)


def solution(mesh):
    finer = Mesh(mesh.devices.reshape(2, 2, Y_SIZE, Z_SIZE, 2), ALL_AXES)
    rows = P(ALL_AXES, None)
    in_specs = (rows, rows, rows, P(ALL_AXES), P(), P(), P())
    return jax.shard_map(body, mesh=finer, in_specs=in_specs, out_specs=rows, check_vma=False)
```

```python
import functools
import math

import jax
import jax.numpy as jnp
import numpy as np
from jax import lax
from jax.experimental import pallas as pl
from jax.experimental.pallas import tpu as pltpu
from jax.sharding import Mesh
from jax.sharding import PartitionSpec as P

ALL_AXES = ("x_hi", "core", "y", "z", "x_lo")
ACROSS = ("x_hi", "x_lo")
X_SIZE, Y_SIZE, Z_SIZE = 4, 4, 8

RUN = 32
TOK = 2 * RUN
D_LAT = 512
HEADS = 8
D_NOPE = 128
D_VAL = 128
ROW = D_LAT + 128
Q_ROW = HEADS * D_NOPE + 512 + 128
OUT_ROW = HEADS * D_VAL + 128
Q_TILE = 2 * X_SIZE * RUN
SPANS = 512

NEGATIVE = -1e30
FLOOR = -1e28
SCALE = 1.4426950408889634 / math.sqrt(D_NOPE + 64)

VMEM = pl.BlockSpec(memory_space=pltpu.VMEM)
SMEM = pl.BlockSpec(memory_space=pltpu.SMEM)


def lanes(rows):
    return lax.broadcasted_iota(jnp.int32, (rows, 128), 1)


def turned(values, cosine, sine, first):
    partner = jnp.where(first, pltpu.roll(values, 96, 1), pltpu.roll(values, 32, 1))
    return values * cosine + partner * jnp.where(first, -sine, sine)


def rows_kernel(pos_ref, low_ref, high_ref, step_ref, qn_ref, qr_ref, kv_ref, gain_ref, key_ref, q_ref):
    lane = lanes(RUN)
    first = lane % 64 < 32
    slot = lax.axis_index("y") * Z_SIZE + lax.axis_index("z")
    turn = jnp.where(pos_ref[0] < pos_ref[RUN], 0, RUN)
    span = (jnp.minimum(pos_ref[0], pos_ref[RUN]) // RUN + 1).astype(jnp.float32)
    step_cos, step_sin = step_ref[0], step_ref[1]
    for half, base_ref in enumerate((low_ref, high_ref)):
        src = pl.ds(pl.multiple_of(turn if half == 0 else RUN - turn, RUN), RUN)
        dst = slice(half * RUN, (half + 1) * RUN)
        base_cos, base_sin = base_ref[0, 0:1], base_ref[0, 1:2]
        cosine = base_cos * step_cos - base_sin * step_sin
        sine = base_sin * step_cos + base_cos * step_sin

        raw = kv_ref[src, :D_LAT].astype(jnp.float32)
        mean_sq = jnp.mean(raw * raw, axis=1, keepdims=True)
        latent = raw * lax.rsqrt(mean_sq + 1e-06) * gain_ref[...]
        key_ref[dst, :D_LAT] = latent.astype(jnp.bfloat16)
        rope = kv_ref[src, D_LAT:].astype(jnp.float32)
        rope = turned(jnp.concatenate([rope, jnp.zeros_like(rope)], axis=1), cosine, sine, first)
        tail = jnp.where(lane == 64 + slot, span, 0.0)
        key_ref[dst, D_LAT:] = jnp.where(lane < 64, rope, tail).astype(jnp.bfloat16)

        q_ref[dst, : HEADS * D_NOPE] = qn_ref[src, :]
        for pair in range(HEADS // 2):
            part = qr_ref[src, pair * 128 : (pair + 1) * 128].astype(jnp.float32)
            at = HEADS * D_NOPE + pair * 128
            q_ref[dst, at : at + 128] = (turned(part, cosine, sine, first) * SCALE).astype(jnp.bfloat16)
        q_ref[dst, Q_ROW - 128 :] = jnp.full((RUN, 128), span, jnp.float32).astype(jnp.bfloat16)


def rotations():
    freqs = np.tile(10000.0 ** (-np.arange(32) / 32.0), 4)
    table = lambda p: np.stack([np.cos(p[:, None] * freqs), np.sin(p[:, None] * freqs)], axis=1)
    spans = table(np.arange(SPANS) * float(RUN)).astype(np.float32)
    steps = table(np.arange(RUN) * 1.0).astype(np.float32).transpose(1, 0, 2)
    return spans, steps


def over_lanes(a, b):
    return lax.dot_general(a, b, (((1,), (1,)), ((), ())), preferred_element_type=jnp.float32)


def expand_kernel(n_keys, *refs):
    key_refs, (uk_ref, uv_ref, k_ref, v_ref, tail_ref) = refs[:n_keys], refs[n_keys:]
    for half in range(2):
        run = slice(half * RUN, (half + 1) * RUN)
        rows = [ref[:, run, :].reshape(-1, ROW) for ref in key_refs]
        rows = jnp.concatenate(rows, axis=0) if n_keys > 1 else rows[0]
        latent = rows[:, :D_LAT]
        tail_ref[half] = rows[:, D_LAT:]
        for pair in range(HEADS // 2):
            cols = slice(pair * 256, (pair + 1) * 256)
            k_ref[half, :, cols] = (over_lanes(latent, uk_ref[cols, :]) * SCALE).astype(jnp.bfloat16)
            w = jnp.concatenate([uv_ref[2 * pair], uv_ref[2 * pair + 1]], axis=1)
            v_ref[half, :, cols] = jnp.dot(latent, w, preferred_element_type=jnp.float32).astype(jnp.bfloat16)


def expand(blocks, w_uk, w_uv):
    n = sum(b.shape[0] for b in blocks) * RUN
    out = lambda width: jax.ShapeDtypeStruct((2, n, width), jnp.bfloat16)
    return pl.pallas_call(
        functools.partial(expand_kernel, len(blocks)),
        in_specs=[VMEM] * (len(blocks) + 2),
        out_specs=[VMEM] * 3,
        out_shape=[out(HEADS * D_NOPE), out(HEADS * D_VAL), out(128)],
        compiler_params=pltpu.CompilerParams(vmem_limit_bytes=14 << 20),
        cost_estimate=pl.CostEstimate(
            flops=4 * n * D_LAT * 2048, bytes_accessed=n * 12000 + (2 << 20), transcendentals=0
        ),
        name="expand",
    )(*blocks, w_uk.reshape(HEADS * D_NOPE, D_LAT), w_uv)


def packed(stats):
    top = stats.astype(jnp.bfloat16)
    rest = stats - top.astype(jnp.float32)
    mid = rest.astype(jnp.bfloat16)
    rest = rest - mid.astype(jnp.float32)
    pieces = top.astype(jnp.float32) + pltpu.roll(mid.astype(jnp.float32), 8, 1)
    return (pieces + pltpu.roll(rest, 16, 1)).astype(jnp.bfloat16)


def unpacked(pieces):
    pieces = pieces.astype(jnp.float32)
    return pieces + pltpu.roll(pieces, 120, 1) + pltpu.roll(pieces, 112, 1)


def attend_kernel(n_chunks, own, *refs):
    near_ref, far_ref = refs[:2]
    k_refs, v_refs, tail_refs = (refs[2 + i * n_chunks : 2 + (i + 1) * n_chunks] for i in range(3))
    outs, lse_scr = refs[2 + 3 * n_chunks : -1], refs[-1]
    lane = lanes(RUN)
    q_refs = [(ref, i) for ref in (near_ref, far_ref) for i in range(X_SIZE)]
    tails = [jnp.concatenate([ref[half] for ref in tail_refs], axis=0) for half in range(2)]
    spans = jnp.max(tails[0].astype(jnp.float32), axis=0, keepdims=True)
    ones = jnp.ones((tails[0].shape[0], 128), jnp.bfloat16)
    row, col = (lax.broadcasted_iota(jnp.int32, (Q_TILE, 128), d) for d in (0, 1))
    later = (row < RUN) & (col < RUN) & (col > row)
    runs = [slice(half * RUN, (half + 1) * RUN) for half in range(2)]
    biases = []
    for half in range(2):
        biases.append([])
        for ref, i in q_refs:
            mine = ref[i, 0:16, Q_ROW - 128 :].astype(jnp.float32)[0:1]
            seen = (spans >= mine) if half else (spans <= mine)
            biases[half].append(jnp.where(seen, 0.0, NEGATIVE))
    lse_scr[...] = jnp.zeros_like(lse_scr)

    def hide(score):
        if not own:
            return score
        return jnp.concatenate([jnp.where(later, NEGATIVE, score[:, :128]), score[:, 128:]], axis=1)

    def pair_of_heads(step, carry):
        at = pl.multiple_of(step * 256, 256)
        rope_at = pl.multiple_of(HEADS * D_NOPE + step * 128, 128)
        nope = [jnp.concatenate([ref[i, run, pl.ds(at, 256)] for ref, i in q_refs], axis=0) for run in runs]
        ropes = [[ref[i, run, pl.ds(rope_at, 128)].astype(jnp.float32) for ref, i in q_refs] for run in runs]
        k_pair = [jnp.concatenate([ref[half, :, pl.ds(at, 256)] for ref in k_refs], axis=0) for half in range(2)]
        v_pair = [jnp.concatenate([ref[half, :, pl.ds(at, 256)] for ref in v_refs], axis=0) for half in range(2)]
        scores = []
        for inner in range(2):
            cols = slice(inner * 128, (inner + 1) * 128)

            def rows_of(half, fill):
                ends = [
                    jnp.where(lane < 64, pltpu.roll(r, 64, 1) if inner else r, f)
                    for r, f in zip(ropes[half], fill)
                ]
                ends = jnp.concatenate(ends, axis=0).astype(jnp.bfloat16)
                return jnp.concatenate([nope[half][:, cols], ends], axis=1)

            keys = [jnp.concatenate([k[:, cols], tail], axis=1) for k, tail in zip(k_pair, tails)]
            both = jnp.concatenate([rows_of(0, biases[0]), rows_of(1, [0.0] * len(q_refs))], axis=0)
            on_low = over_lanes(both, keys[0])
            on_high = over_lanes(rows_of(1, biases[1]), keys[1])
            scores.append((hide(on_low[:Q_TILE]), on_low[Q_TILE:], hide(on_high)))
        peaks = []
        for low, middle, high in scores:
            top = [jnp.max(s, axis=1, keepdims=True) for s in (low, middle, high)]
            peaks.append((jnp.maximum(top[0], FLOOR), jnp.maximum(top[1], jnp.maximum(top[2], FLOOR))))
        weights = []
        for (low, middle, high), (p_low, p_high) in zip(scores, peaks):
            on_low = [jnp.exp2(low - p_low).astype(jnp.bfloat16), jnp.exp2(middle - p_high).astype(jnp.bfloat16)]
            weights.append((jnp.concatenate(on_low, axis=0), jnp.exp2(high - p_high).astype(jnp.bfloat16)))
        sums = []
        for inner, (on_low, on_high) in enumerate(weights):
            cols = slice(inner * 128, (inner + 1) * 128)
            values = [jnp.concatenate([v[:, cols], ones], axis=1) for v in v_pair]
            a = jnp.dot(on_low, values[0], preferred_element_type=jnp.float32)
            b = jnp.dot(on_high, values[1], preferred_element_type=jnp.float32)
            sums.append((a[:Q_TILE], a[Q_TILE:] + b))
        for inner in range(2):
            head_at = pl.multiple_of(step * 256 + inner * 128, 128)
            for half in range(2):
                added, peak = sums[inner][half], peaks[inner][half]
                some = added[:, D_VAL:] > 0.0
                total = jnp.where(some, added[:, D_VAL:], 1.0)
                result = (added[:, :D_VAL] / total).astype(jnp.bfloat16)
                lse = jnp.where(some, peak + jnp.log2(total), NEGATIVE)
                for i in range(2 * X_SIZE):
                    rows = slice(i * RUN, (i + 1) * RUN)
                    outs[i // X_SIZE][i % X_SIZE, runs[half], pl.ds(head_at, 128)] = result[rows]
                    held = lse_scr[i, runs[half], :]
                    lse_scr[i, runs[half], :] = jnp.where(lane == 2 * step + inner, lse[rows], held)
        return carry

    lax.fori_loop(0, HEADS // 2, pair_of_heads, 0)
    for i in range(2 * X_SIZE):
        outs[i // X_SIZE][i % X_SIZE, :, HEADS * D_VAL :] = packed(lse_scr[i])


def attend(near, far, chunks, own):
    ks, vs, tails = zip(*chunks)
    out = jax.ShapeDtypeStruct((X_SIZE, TOK, OUT_ROW), jnp.bfloat16)
    return pl.pallas_call(
        functools.partial(attend_kernel, len(chunks), own),
        in_specs=[VMEM] * (2 + 3 * len(chunks)),
        out_specs=[VMEM] * 2,
        out_shape=[out, out],
        scratch_shapes=[pltpu.VMEM((2 * X_SIZE, TOK, 128), jnp.float32)],
        compiler_params=pltpu.CompilerParams(vmem_limit_bytes=22 << 20),
        cost_estimate=pl.CostEstimate(
            flops=10**7 * sum(a.shape[1] for a in ks), bytes_accessed=8 << 20, transcendentals=3 * 10**6
        ),
        name="attend",
    )(near, far, *ks, *vs, *tails)


def mix(parts, shares, run, h):
    cols = slice(h * D_VAL, (h + 1) * D_VAL)
    terms = [p[run, cols].astype(jnp.float32) * s[run, h : h + 1] for p, s in zip(parts, shares)]
    return functools.reduce(jnp.add, terms)


def merge_kernel(n_parts, *refs):
    for i, out_ref in enumerate(refs[n_parts:], 1):
        parts = [ref.at[i] for ref in refs[:n_parts]]
        stats = [unpacked(p[:, HEADS * D_VAL :]) for p in parts]
        best = functools.reduce(jnp.maximum, stats)
        shares = [jnp.exp2(s - best) for s in stats]
        whole = functools.reduce(jnp.add, shares)
        used = lanes(TOK) < HEADS
        out_ref[:, HEADS * D_VAL :] = packed(jnp.where(used, best + jnp.log2(whole), 0.0))
        shares = [s / whole for s in shares]
        for h in range(HEADS):
            out_ref[:, h * D_VAL : (h + 1) * D_VAL] = mix(parts, shares, slice(0, TOK), h).astype(jnp.bfloat16)


def combine_kernel(n_local, pos_ref, *refs):
    parts, out_ref = [ref.at[0] for ref in refs[:n_local]] + list(refs[n_local:-1]), refs[-1]
    stats = [unpacked(p[:, HEADS * D_VAL :]) for p in parts]
    best = functools.reduce(jnp.maximum, stats)
    shares = [jnp.exp2(s - best) for s in stats]
    whole = functools.reduce(jnp.add, shares)
    shares = [s / whole for s in shares]
    turn = jnp.where(pos_ref[0] < pos_ref[RUN], 0, RUN)
    for half in range(2):
        dst = pl.ds(pl.multiple_of(turn if half == 0 else RUN - turn, RUN), RUN)
        run = slice(half * RUN, (half + 1) * RUN)
        for h in range(HEADS):
            out_ref[dst, h * D_VAL : (h + 1) * D_VAL] = mix(parts, shares, run, h).astype(jnp.bfloat16)


def shift(size, by):
    return [(i, (i + by) % size) for i in range(size)]


def body(q_nope, q_rope, kv_compressed, token_pos, kv_gain, w_uk, w_uv):
    spans, steps = rotations()
    low_span = lambda i, pos: (jnp.minimum(pos[0], pos[RUN]) // RUN, 0, 0)
    high_span = lambda i, pos: (jnp.maximum(pos[0], pos[RUN]) // RUN, 0, 0)
    whole = lambda shape: pl.BlockSpec(shape, lambda i, pos: (0,) * len(shape))
    key_rows, q_rows = pl.pallas_call(
        rows_kernel,
        grid_spec=pltpu.PrefetchScalarGridSpec(
            num_scalar_prefetch=1,
            grid=(1,),
            in_specs=[
                pl.BlockSpec((1, 2, 128), low_span),
                pl.BlockSpec((1, 2, 128), high_span),
                whole((2, RUN, 128)),
                whole(q_nope.shape),
                whole(q_rope.shape),
                whole(kv_compressed.shape),
                whole((1, D_LAT)),
            ],
            out_specs=[whole((TOK, ROW)), whole((TOK, Q_ROW))],
        ),
        out_shape=[
            jax.ShapeDtypeStruct((TOK, ROW), jnp.bfloat16),
            jax.ShapeDtypeStruct((TOK, Q_ROW), jnp.bfloat16),
        ],
        name="rows",
    )(token_pos, spans, spans, steps, q_nope, q_rope, kv_compressed, kv_gain[None, :])

    swap = lambda block: lax.ppermute(block, "core", [(0, 1), (1, 0)])
    across = lambda block, by: lax.ppermute(block, ACROSS, shift(X_SIZE, by))
    along = lambda block, by: lax.ppermute(block, "z", shift(Z_SIZE, by))

    along_y = [lax.ppermute(key_rows, "y", shift(Y_SIZE, by)) for by in (1, -1, 2)]
    mine = jnp.stack([key_rows] + along_y)
    from_left = across(q_rows, 1)
    mine, q_rows, from_left = lax.optimization_barrier((mine, q_rows, from_left))

    up, down = along(mine, 1), along(mine, -1)
    opposite = across(q_rows, 2)
    first = [expand([mine], w_uk, w_uv)]
    up, down, opposite, q_rows, first = lax.optimization_barrier((up, down, opposite, q_rows, first))

    blocks = [up, down]
    up, down = along(up, 1), along(down, -1)
    from_right = across(q_rows, -1)
    first.append(expand(blocks, w_uk, w_uv))
    up, down, from_right, first = lax.optimization_barrier((up, down, from_right, first))

    blocks = [up, down]
    up, down = along(up, 1), along(down, -1)
    near = jnp.stack([q_rows, from_left, from_right, opposite])
    far = swap(near)
    second = [expand(blocks, w_uk, w_uv)]
    partials = [attend(near, far, first, True)]
    up, down, second, partials = lax.optimization_barrier((up, down, second, partials))

    blocks = [up, down]
    half = Y_SIZE // 2
    up, down = along(up[:half], 1), along(down[half:], -1)
    crossed = [swap(partials[0][1])]
    third = [expand(blocks, w_uk, w_uv)]
    partials.append(attend(near, far, second, False))
    up, down, third, partials, crossed = lax.optimization_barrier((up, down, third, partials, crossed))

    third.append(expand([up, down], w_uk, w_uv))
    crossed.append(swap(partials[1][1]))
    partials.append(attend(near, far, third, False))
    crossed.append(swap(partials[2][1]))

    local = [p[0] for p in partials] + crossed
    part = jax.ShapeDtypeStruct((TOK, OUT_ROW), jnp.bfloat16)
    merged = pl.pallas_call(
        functools.partial(merge_kernel, len(local)),
        in_specs=[VMEM] * len(local),
        out_specs=[VMEM] * 3,
        out_shape=[part] * 3,
        compiler_params=pltpu.CompilerParams(vmem_limit_bytes=8 << 20),
        name="merge",
    )(*local)
    back = [across(m, by) for m, by in zip(merged, (-1, 1, 2))]
    return pl.pallas_call(
        functools.partial(combine_kernel, len(local)),
        in_specs=[SMEM] + [VMEM] * (len(local) + 3),
        out_specs=VMEM,
        out_shape=jax.ShapeDtypeStruct((TOK, HEADS * D_VAL), jnp.bfloat16),
        compiler_params=pltpu.CompilerParams(vmem_limit_bytes=8 << 20),
        name="combine",
    )(token_pos, *local, *back)


def solution(mesh):
    finer = Mesh(mesh.devices.reshape(2, 2, Y_SIZE, Z_SIZE, 2), ALL_AXES)
    rows = P(ALL_AXES, None)
    in_specs = (rows, rows, rows, P(ALL_AXES), P(), P(), P())
    return jax.shard_map(body, mesh=finer, in_specs=in_specs, out_specs=rows, check_vma=False)
```

```python
import functools
import math

import jax
import jax.numpy as jnp
import numpy as np
from jax import lax
from jax.experimental import pallas as pl
from jax.experimental.pallas import tpu as pltpu
from jax.sharding import Mesh
from jax.sharding import PartitionSpec as P

ALL_AXES = ("x_hi", "core", "y", "z", "x_lo")
ACROSS = ("x_hi", "x_lo")
X_SIZE, Y_SIZE, Z_SIZE = 4, 4, 8

RUN = 32
TOK = 2 * RUN
D_LAT = 512
HEADS = 8
D_NOPE = 128
D_VAL = 128
ROW = D_LAT + 128
Q_ROW = HEADS * D_NOPE + 512 + 128
OUT_ROW = HEADS * D_VAL + 128
Q_TILE = 2 * X_SIZE * RUN
SPANS = 512

NEGATIVE = -1e30
FLOOR = -1e28
SCALE = 1.4426950408889634 / math.sqrt(D_NOPE + 64)

VMEM = pl.BlockSpec(memory_space=pltpu.VMEM)
SMEM = pl.BlockSpec(memory_space=pltpu.SMEM)


def lanes(rows):
    return lax.broadcasted_iota(jnp.int32, (rows, 128), 1)


def turned(values, cosine, sine, first):
    partner = jnp.where(first, pltpu.roll(values, 96, 1), pltpu.roll(values, 32, 1))
    return values * cosine + partner * jnp.where(first, -sine, sine)


def rows_kernel(pos_ref, low_ref, high_ref, step_ref, qn_ref, qr_ref, kv_ref, gain_ref, key_ref, q_ref):
    lane = lanes(RUN)
    first = lane % 64 < 32
    slot = lax.axis_index("y") * Z_SIZE + lax.axis_index("z")
    turn = jnp.where(pos_ref[0] < pos_ref[RUN], 0, RUN)
    span = (jnp.minimum(pos_ref[0], pos_ref[RUN]) // RUN + 1).astype(jnp.float32)
    step_cos, step_sin = step_ref[0], step_ref[1]
    for half, base_ref in enumerate((low_ref, high_ref)):
        src = pl.ds(pl.multiple_of(turn if half == 0 else RUN - turn, RUN), RUN)
        dst = slice(half * RUN, (half + 1) * RUN)
        base_cos, base_sin = base_ref[0, 0:1], base_ref[0, 1:2]
        cosine = base_cos * step_cos - base_sin * step_sin
        sine = base_sin * step_cos + base_cos * step_sin

        raw = kv_ref[src, :D_LAT].astype(jnp.float32)
        mean_sq = jnp.mean(raw * raw, axis=1, keepdims=True)
        latent = raw * lax.rsqrt(mean_sq + 1e-06) * gain_ref[...]
        key_ref[dst, :D_LAT] = latent.astype(jnp.bfloat16)
        rope = kv_ref[src, D_LAT:].astype(jnp.float32)
        rope = turned(jnp.concatenate([rope, jnp.zeros_like(rope)], axis=1), cosine, sine, first)
        tail = jnp.where(lane == 64 + slot, span, 0.0)
        key_ref[dst, D_LAT:] = jnp.where(lane < 64, rope, tail).astype(jnp.bfloat16)

        q_ref[dst, : HEADS * D_NOPE] = qn_ref[src, :]
        for pair in range(HEADS // 2):
            part = qr_ref[src, pair * 128 : (pair + 1) * 128].astype(jnp.float32)
            at = HEADS * D_NOPE + pair * 128
            q_ref[dst, at : at + 128] = (turned(part, cosine, sine, first) * SCALE).astype(jnp.bfloat16)
        q_ref[dst, Q_ROW - 128 :] = jnp.full((RUN, 128), span, jnp.float32).astype(jnp.bfloat16)


def rotations():
    freqs = np.tile(10000.0 ** (-np.arange(32) / 32.0), 4)
    table = lambda p: np.stack([np.cos(p[:, None] * freqs), np.sin(p[:, None] * freqs)], axis=1)
    spans = table(np.arange(SPANS) * float(RUN)).astype(np.float32)
    steps = table(np.arange(RUN) * 1.0).astype(np.float32).transpose(1, 0, 2)
    return spans, steps


def over_lanes(a, b):
    return lax.dot_general(a, b, (((1,), (1,)), ((), ())), preferred_element_type=jnp.float32)


def expand_kernel(n_keys, *refs):
    key_refs, (uk_ref, uv_ref, k_ref, v_ref, tail_ref) = refs[:n_keys], refs[n_keys:]
    for half in range(2):
        run = slice(half * RUN, (half + 1) * RUN)
        rows = [ref[:, run, :].reshape(-1, ROW) for ref in key_refs]
        rows = jnp.concatenate(rows, axis=0) if n_keys > 1 else rows[0]
        latent = rows[:, :D_LAT]
        tail_ref[half] = rows[:, D_LAT:]
        for pair in range(HEADS // 2):
            cols = slice(pair * 256, (pair + 1) * 256)
            k_ref[half, :, cols] = (over_lanes(latent, uk_ref[cols, :]) * SCALE).astype(jnp.bfloat16)
            w = jnp.concatenate([uv_ref[2 * pair], uv_ref[2 * pair + 1]], axis=1)
            v_ref[half, :, cols] = jnp.dot(latent, w, preferred_element_type=jnp.float32).astype(jnp.bfloat16)


def expand(blocks, w_uk, w_uv):
    n = sum(b.shape[0] for b in blocks) * RUN
    out = lambda width: jax.ShapeDtypeStruct((2, n, width), jnp.bfloat16)
    return pl.pallas_call(
        functools.partial(expand_kernel, len(blocks)),
        in_specs=[VMEM] * (len(blocks) + 2),
        out_specs=[VMEM] * 3,
        out_shape=[out(HEADS * D_NOPE), out(HEADS * D_VAL), out(128)],
        compiler_params=pltpu.CompilerParams(vmem_limit_bytes=14 << 20),
        cost_estimate=pl.CostEstimate(
            flops=4 * n * D_LAT * 2048, bytes_accessed=n * 12000 + (2 << 20), transcendentals=0
        ),
        name="expand",
    )(*blocks, w_uk.reshape(HEADS * D_NOPE, D_LAT), w_uv)


def packed(stats):
    top = stats.astype(jnp.bfloat16)
    rest = stats - top.astype(jnp.float32)
    mid = rest.astype(jnp.bfloat16)
    rest = rest - mid.astype(jnp.float32)
    pieces = top.astype(jnp.float32) + pltpu.roll(mid.astype(jnp.float32), 8, 1)
    return (pieces + pltpu.roll(rest, 16, 1)).astype(jnp.bfloat16)


def unpacked(pieces):
    pieces = pieces.astype(jnp.float32)
    return pieces + pltpu.roll(pieces, 120, 1) + pltpu.roll(pieces, 112, 1)


def attend_kernel(n_chunks, own, *refs):
    near_ref, far_ref = refs[:2]
    k_refs, v_refs, tail_refs = (refs[2 + i * n_chunks : 2 + (i + 1) * n_chunks] for i in range(3))
    outs, lse_scr = refs[2 + 3 * n_chunks : -1], refs[-1]
    lane = lanes(RUN)
    q_refs = [(ref, i) for ref in (near_ref, far_ref) for i in range(X_SIZE)]
    tails = [jnp.concatenate([ref[half] for ref in tail_refs], axis=0) for half in range(2)]
    spans = jnp.max(tails[0].astype(jnp.float32), axis=0, keepdims=True)
    ones = jnp.ones((tails[0].shape[0], 128), jnp.bfloat16)
    row, col = (lax.broadcasted_iota(jnp.int32, (Q_TILE, 128), d) for d in (0, 1))
    later = (row < RUN) & (col < RUN) & (col > row)
    runs = [slice(half * RUN, (half + 1) * RUN) for half in range(2)]
    biases = []
    for half in range(2):
        biases.append([])
        for ref, i in q_refs:
            mine = ref[i, 0:16, Q_ROW - 128 :].astype(jnp.float32)[0:1]
            seen = (spans >= mine) if half else (spans <= mine)
            biases[half].append(jnp.where(seen, 0.0, NEGATIVE))
    lse_scr[...] = jnp.zeros_like(lse_scr)

    def hide(score):
        if not own:
            return score
        return jnp.concatenate([jnp.where(later, NEGATIVE, score[:, :128]), score[:, 128:]], axis=1)

    def pair_of_heads(step, carry):
        at = pl.multiple_of(step * 256, 256)
        rope_at = pl.multiple_of(HEADS * D_NOPE + step * 128, 128)
        nope = [jnp.concatenate([ref[i, run, pl.ds(at, 256)] for ref, i in q_refs], axis=0) for run in runs]
        ropes = [[ref[i, run, pl.ds(rope_at, 128)].astype(jnp.float32) for ref, i in q_refs] for run in runs]
        k_pair = [jnp.concatenate([ref[half, :, pl.ds(at, 256)] for ref in k_refs], axis=0) for half in range(2)]
        v_pair = [jnp.concatenate([ref[half, :, pl.ds(at, 256)] for ref in v_refs], axis=0) for half in range(2)]
        scores = []
        for inner in range(2):
            cols = slice(inner * 128, (inner + 1) * 128)

            def rows_of(half, fill):
                ends = [
                    jnp.where(lane < 64, pltpu.roll(r, 64, 1) if inner else r, f)
                    for r, f in zip(ropes[half], fill)
                ]
                ends = jnp.concatenate(ends, axis=0).astype(jnp.bfloat16)
                return jnp.concatenate([nope[half][:, cols], ends], axis=1)

            keys = [jnp.concatenate([k[:, cols], tail], axis=1) for k, tail in zip(k_pair, tails)]
            both = jnp.concatenate([rows_of(0, biases[0]), rows_of(1, [0.0] * len(q_refs))], axis=0)
            on_low = over_lanes(both, keys[0])
            on_high = over_lanes(rows_of(1, biases[1]), keys[1])
            scores.append((hide(on_low[:Q_TILE]), on_low[Q_TILE:], hide(on_high)))
        peaks = []
        for low, middle, high in scores:
            top = [jnp.max(s, axis=1, keepdims=True) for s in (low, middle, high)]
            peaks.append((jnp.maximum(top[0], FLOOR), jnp.maximum(top[1], jnp.maximum(top[2], FLOOR))))
        weights = []
        for (low, middle, high), (p_low, p_high) in zip(scores, peaks):
            on_low = [jnp.exp2(low - p_low).astype(jnp.bfloat16), jnp.exp2(middle - p_high).astype(jnp.bfloat16)]
            weights.append((jnp.concatenate(on_low, axis=0), jnp.exp2(high - p_high).astype(jnp.bfloat16)))
        sums = []
        for inner, (on_low, on_high) in enumerate(weights):
            cols = slice(inner * 128, (inner + 1) * 128)
            values = [jnp.concatenate([v[:, cols], ones], axis=1) for v in v_pair]
            a = jnp.dot(on_low, values[0], preferred_element_type=jnp.float32)
            b = jnp.dot(on_high, values[1], preferred_element_type=jnp.float32)
            sums.append((a[:Q_TILE], a[Q_TILE:] + b))
        for inner in range(2):
            head_at = pl.multiple_of(step * 256 + inner * 128, 128)
            for half in range(2):
                added, peak = sums[inner][half], peaks[inner][half]
                some = added[:, D_VAL:] > 0.0
                total = jnp.where(some, added[:, D_VAL:], 1.0)
                result = (added[:, :D_VAL] / total).astype(jnp.bfloat16)
                lse = jnp.where(some, peak + jnp.log2(total), NEGATIVE)
                for i in range(2 * X_SIZE):
                    rows = slice(i * RUN, (i + 1) * RUN)
                    outs[i // X_SIZE][i % X_SIZE, runs[half], pl.ds(head_at, 128)] = result[rows]
                    held = lse_scr[i, runs[half], :]
                    lse_scr[i, runs[half], :] = jnp.where(lane == 2 * step + inner, lse[rows], held)
        return carry

    lax.fori_loop(0, HEADS // 2, pair_of_heads, 0)
    for i in range(2 * X_SIZE):
        outs[i // X_SIZE][i % X_SIZE, :, HEADS * D_VAL :] = packed(lse_scr[i])


def attend(near, far, chunks, own):
    ks, vs, tails = zip(*chunks)
    out = jax.ShapeDtypeStruct((X_SIZE, TOK, OUT_ROW), jnp.bfloat16)
    return pl.pallas_call(
        functools.partial(attend_kernel, len(chunks), own),
        in_specs=[VMEM] * (2 + 3 * len(chunks)),
        out_specs=[VMEM] * 2,
        out_shape=[out, out],
        scratch_shapes=[pltpu.VMEM((2 * X_SIZE, TOK, 128), jnp.float32)],
        compiler_params=pltpu.CompilerParams(vmem_limit_bytes=22 << 20),
        cost_estimate=pl.CostEstimate(
            flops=10**7 * sum(a.shape[1] for a in ks), bytes_accessed=8 << 20, transcendentals=3 * 10**6
        ),
        name="attend",
    )(near, far, *ks, *vs, *tails)


def mix(parts, shares, run, h):
    cols = slice(h * D_VAL, (h + 1) * D_VAL)
    terms = [p[run, cols].astype(jnp.float32) * s[run, h : h + 1] for p, s in zip(parts, shares)]
    return functools.reduce(jnp.add, terms)


def merge_kernel(n_parts, which, *refs):
    for i, out_ref in zip(which, refs[n_parts:]):
        parts = [ref.at[i] for ref in refs[:n_parts]]
        stats = [unpacked(p[:, HEADS * D_VAL :]) for p in parts]
        best = functools.reduce(jnp.maximum, stats)
        shares = [jnp.exp2(s - best) for s in stats]
        whole = functools.reduce(jnp.add, shares)
        used = lanes(TOK) < HEADS
        out_ref[:, HEADS * D_VAL :] = packed(jnp.where(used, best + jnp.log2(whole), 0.0))
        shares = [s / whole for s in shares]
        for h in range(HEADS):
            out_ref[:, h * D_VAL : (h + 1) * D_VAL] = mix(parts, shares, slice(0, TOK), h).astype(jnp.bfloat16)


def merge(parts, which):
    return pl.pallas_call(
        functools.partial(merge_kernel, len(parts), which),
        in_specs=[VMEM] * len(parts),
        out_specs=[VMEM] * len(which),
        out_shape=[jax.ShapeDtypeStruct((TOK, OUT_ROW), jnp.bfloat16)] * len(which),
        compiler_params=pltpu.CompilerParams(vmem_limit_bytes=8 << 20),
        name="merge",
    )(*parts)


def combine_kernel(n_local, pos_ref, *refs):
    parts, out_ref = [ref.at[0] for ref in refs[:n_local]] + list(refs[n_local:-1]), refs[-1]
    stats = [unpacked(p[:, HEADS * D_VAL :]) for p in parts]
    best = functools.reduce(jnp.maximum, stats)
    shares = [jnp.exp2(s - best) for s in stats]
    whole = functools.reduce(jnp.add, shares)
    shares = [s / whole for s in shares]
    turn = jnp.where(pos_ref[0] < pos_ref[RUN], 0, RUN)
    for half in range(2):
        dst = pl.ds(pl.multiple_of(turn if half == 0 else RUN - turn, RUN), RUN)
        run = slice(half * RUN, (half + 1) * RUN)
        for h in range(HEADS):
            out_ref[dst, h * D_VAL : (h + 1) * D_VAL] = mix(parts, shares, run, h).astype(jnp.bfloat16)


def shift(size, by):
    return [(i, (i + by) % size) for i in range(size)]


def body(q_nope, q_rope, kv_compressed, token_pos, kv_gain, w_uk, w_uv):
    spans, steps = rotations()
    low_span = lambda i, pos: (jnp.minimum(pos[0], pos[RUN]) // RUN, 0, 0)
    high_span = lambda i, pos: (jnp.maximum(pos[0], pos[RUN]) // RUN, 0, 0)
    whole = lambda shape: pl.BlockSpec(shape, lambda i, pos: (0,) * len(shape))
    key_rows, q_rows = pl.pallas_call(
        rows_kernel,
        grid_spec=pltpu.PrefetchScalarGridSpec(
            num_scalar_prefetch=1,
            grid=(1,),
            in_specs=[
                pl.BlockSpec((1, 2, 128), low_span),
                pl.BlockSpec((1, 2, 128), high_span),
                whole((2, RUN, 128)),
                whole(q_nope.shape),
                whole(q_rope.shape),
                whole(kv_compressed.shape),
                whole((1, D_LAT)),
            ],
            out_specs=[whole((TOK, ROW)), whole((TOK, Q_ROW))],
        ),
        out_shape=[
            jax.ShapeDtypeStruct((TOK, ROW), jnp.bfloat16),
            jax.ShapeDtypeStruct((TOK, Q_ROW), jnp.bfloat16),
        ],
        name="rows",
    )(token_pos, spans, spans, steps, q_nope, q_rope, kv_compressed, kv_gain[None, :])

    swap = lambda block: lax.ppermute(block, "core", [(0, 1), (1, 0)])
    across = lambda block, by: lax.ppermute(block, ACROSS, shift(X_SIZE, by))
    along = lambda block, by: lax.ppermute(block, "z", shift(Z_SIZE, by))

    along_y = [lax.ppermute(key_rows, "y", shift(Y_SIZE, by)) for by in (1, -1, 2)]
    mine = jnp.stack([key_rows] + along_y)
    from_left = across(q_rows, 1)
    mine, q_rows, from_left = lax.optimization_barrier((mine, q_rows, from_left))

    up, down = along(mine, 1), along(mine, -1)
    opposite = across(q_rows, 2)
    first = [expand([mine], w_uk, w_uv)]
    up, down, opposite, q_rows, first = lax.optimization_barrier((up, down, opposite, q_rows, first))

    blocks = [up, down]
    up, down = along(up, 1), along(down, -1)
    from_right = across(q_rows, -1)
    first.append(expand(blocks, w_uk, w_uv))
    up, down, from_right, first = lax.optimization_barrier((up, down, from_right, first))

    blocks = [up, down]
    up, down = along(up, 1), along(down, -1)
    near = jnp.stack([q_rows, from_left, from_right, opposite])
    far = swap(near)
    second = [expand(blocks, w_uk, w_uv)]
    partials = [attend(near, far, first, True)]
    up, down, second, partials = lax.optimization_barrier((up, down, second, partials))

    blocks = [up, down]
    half = Y_SIZE // 2
    up, down = along(up[:half], 1), along(down[half:], -1)
    second.append(expand(blocks, w_uk, w_uv))
    partials.append(attend(near, far, second, False))
    up, down, partials = lax.optimization_barrier((up, down, partials))

    crossed = [swap(p[1]) for p in partials]
    partials.append(attend(near, far, [expand([up, down], w_uk, w_uv)], False))
    crossed.append(swap(partials[2][1]))

    local = [p[0] for p in partials] + crossed
    opposite, = merge(local, [3])
    local, opposite = lax.optimization_barrier((local, opposite))
    right, left = merge(local, [1, 2])
    back = [across(m, by) for m, by in ((opposite, 2), (right, -1), (left, 1))]
    return pl.pallas_call(
        functools.partial(combine_kernel, len(local)),
        in_specs=[SMEM] + [VMEM] * (len(local) + 3),
        out_specs=VMEM,
        out_shape=jax.ShapeDtypeStruct((TOK, HEADS * D_VAL), jnp.bfloat16),
        compiler_params=pltpu.CompilerParams(vmem_limit_bytes=8 << 20),
        name="combine",
    )(token_pos, *local, *back)


def solution(mesh):
    finer = Mesh(mesh.devices.reshape(2, 2, Y_SIZE, Z_SIZE, 2), ALL_AXES)
    rows = P(ALL_AXES, None)
    in_specs = (rows, rows, rows, P(ALL_AXES), P(), P(), P())
    return jax.shard_map(body, mesh=finer, in_specs=in_specs, out_specs=rows, check_vma=False)
```

```python
import functools
import math

import jax
import jax.numpy as jnp
import numpy as np
from jax import lax
from jax.experimental import pallas as pl
from jax.experimental.pallas import tpu as pltpu
from jax.sharding import Mesh
from jax.sharding import PartitionSpec as P

ALL_AXES = ("x_hi", "core", "y", "z", "x_lo")
ACROSS = ("x_hi", "x_lo")
X_SIZE, Y_SIZE, Z_SIZE = 4, 4, 8

RUN = 32
TOK = 2 * RUN
D_LAT = 512
HEADS = 8
D_NOPE = 128
D_VAL = 128
ROW = D_LAT + 128
Q_ROW = HEADS * D_NOPE + 512 + 128
OUT_ROW = HEADS * D_VAL + 128
Q_TILE = 2 * X_SIZE * RUN
SPANS = 512

NEGATIVE = -1e30
FLOOR = -1e28
SCALE = 1.4426950408889634 / math.sqrt(D_NOPE + 64)

VMEM = pl.BlockSpec(memory_space=pltpu.VMEM)
SMEM = pl.BlockSpec(memory_space=pltpu.SMEM)


def lanes(rows):
    return lax.broadcasted_iota(jnp.int32, (rows, 128), 1)


def turned(values, cosine, sine, first):
    partner = jnp.where(first, pltpu.roll(values, 96, 1), pltpu.roll(values, 32, 1))
    return values * cosine + partner * jnp.where(first, -sine, sine)


def rows_kernel(pos_ref, low_ref, high_ref, step_ref, qn_ref, qr_ref, kv_ref, gain_ref, key_ref, q_ref):
    lane = lanes(RUN)
    first = lane % 64 < 32
    slot = lax.axis_index("y") * Z_SIZE + lax.axis_index("z")
    turn = jnp.where(pos_ref[0] < pos_ref[RUN], 0, RUN)
    span = (jnp.minimum(pos_ref[0], pos_ref[RUN]) // RUN + 1).astype(jnp.float32)
    step_cos, step_sin = step_ref[0], step_ref[1]
    for half, base_ref in enumerate((low_ref, high_ref)):
        src = pl.ds(pl.multiple_of(turn if half == 0 else RUN - turn, RUN), RUN)
        dst = slice(half * RUN, (half + 1) * RUN)
        base_cos, base_sin = base_ref[0, 0:1], base_ref[0, 1:2]
        cosine = base_cos * step_cos - base_sin * step_sin
        sine = base_sin * step_cos + base_cos * step_sin

        raw = kv_ref[src, :D_LAT].astype(jnp.float32)
        mean_sq = jnp.mean(raw * raw, axis=1, keepdims=True)
        latent = raw * lax.rsqrt(mean_sq + 1e-06) * gain_ref[...]
        key_ref[dst, :D_LAT] = latent.astype(jnp.bfloat16)
        rope = kv_ref[src, D_LAT:].astype(jnp.float32)
        rope = turned(jnp.concatenate([rope, jnp.zeros_like(rope)], axis=1), cosine, sine, first)
        tail = jnp.where(lane == 64 + slot, span, 0.0)
        key_ref[dst, D_LAT:] = jnp.where(lane < 64, rope, tail).astype(jnp.bfloat16)

        q_ref[dst, : HEADS * D_NOPE] = qn_ref[src, :]
        for pair in range(HEADS // 2):
            part = qr_ref[src, pair * 128 : (pair + 1) * 128].astype(jnp.float32)
            at = HEADS * D_NOPE + pair * 128
            q_ref[dst, at : at + 128] = (turned(part, cosine, sine, first) * SCALE).astype(jnp.bfloat16)
        q_ref[dst, Q_ROW - 128 :] = jnp.full((RUN, 128), span, jnp.float32).astype(jnp.bfloat16)


def rotations():
    freqs = np.tile(10000.0 ** (-np.arange(32) / 32.0), 4)
    table = lambda p: np.stack([np.cos(p[:, None] * freqs), np.sin(p[:, None] * freqs)], axis=1)
    spans = table(np.arange(SPANS) * float(RUN)).astype(np.float32)
    steps = table(np.arange(RUN) * 1.0).astype(np.float32).transpose(1, 0, 2)
    return spans, steps


def over_lanes(a, b):
    return lax.dot_general(a, b, (((1,), (1,)), ((), ())), preferred_element_type=jnp.float32)


def expand_kernel(n_keys, *refs):
    key_refs, (uk_ref, uv_ref, k_ref, v_ref, tail_ref) = refs[:n_keys], refs[n_keys:]
    for half in range(2):
        run = slice(half * RUN, (half + 1) * RUN)
        rows = [ref[:, run, :].reshape(-1, ROW) for ref in key_refs]
        rows = jnp.concatenate(rows, axis=0) if n_keys > 1 else rows[0]
        latent = rows[:, :D_LAT]
        tail_ref[half] = rows[:, D_LAT:]
        for pair in range(HEADS // 2):
            cols = slice(pair * 256, (pair + 1) * 256)
            k_ref[half, :, cols] = (over_lanes(latent, uk_ref[cols, :]) * SCALE).astype(jnp.bfloat16)
            w = jnp.concatenate([uv_ref[2 * pair], uv_ref[2 * pair + 1]], axis=1)
            v_ref[half, :, cols] = jnp.dot(latent, w, preferred_element_type=jnp.float32).astype(jnp.bfloat16)


def expand(blocks, w_uk, w_uv):
    n = sum(b.shape[0] for b in blocks) * RUN
    out = lambda width: jax.ShapeDtypeStruct((2, n, width), jnp.bfloat16)
    return pl.pallas_call(
        functools.partial(expand_kernel, len(blocks)),
        in_specs=[VMEM] * (len(blocks) + 2),
        out_specs=[VMEM] * 3,
        out_shape=[out(HEADS * D_NOPE), out(HEADS * D_VAL), out(128)],
        compiler_params=pltpu.CompilerParams(vmem_limit_bytes=14 << 20),
        cost_estimate=pl.CostEstimate(
            flops=4 * n * D_LAT * 2048, bytes_accessed=n * 12000 + (2 << 20), transcendentals=0
        ),
        name="expand",
    )(*blocks, w_uk.reshape(HEADS * D_NOPE, D_LAT), w_uv)


def packed(stats):
    top = stats.astype(jnp.bfloat16)
    rest = stats - top.astype(jnp.float32)
    mid = rest.astype(jnp.bfloat16)
    rest = rest - mid.astype(jnp.float32)
    pieces = top.astype(jnp.float32) + pltpu.roll(mid.astype(jnp.float32), 8, 1)
    return (pieces + pltpu.roll(rest, 16, 1)).astype(jnp.bfloat16)


def unpacked(pieces):
    pieces = pieces.astype(jnp.float32)
    return pieces + pltpu.roll(pieces, 120, 1) + pltpu.roll(pieces, 112, 1)


def attend_kernel(n_chunks, own, *refs):
    near_ref, far_ref = refs[:2]
    k_refs, v_refs, tail_refs = (refs[2 + i * n_chunks : 2 + (i + 1) * n_chunks] for i in range(3))
    outs, lse_scr = refs[2 + 3 * n_chunks : -1], refs[-1]
    lane = lanes(RUN)
    q_refs = [(ref, i) for ref in (near_ref, far_ref) for i in range(X_SIZE)]
    tails = [jnp.concatenate([ref[half] for ref in tail_refs], axis=0) for half in range(2)]
    spans = jnp.max(tails[0].astype(jnp.float32), axis=0, keepdims=True)
    ones = jnp.ones((tails[0].shape[0], 128), jnp.bfloat16)
    row, col = (lax.broadcasted_iota(jnp.int32, (Q_TILE, 128), d) for d in (0, 1))
    later = (row < RUN) & (col < RUN) & (col > row)
    runs = [slice(half * RUN, (half + 1) * RUN) for half in range(2)]
    biases = []
    for half in range(2):
        biases.append([])
        for ref, i in q_refs:
            mine = ref[i, 0:16, Q_ROW - 128 :].astype(jnp.float32)[0:1]
            seen = (spans >= mine) if half else (spans <= mine)
            biases[half].append(jnp.where(seen, 0.0, NEGATIVE))
    lse_scr[...] = jnp.zeros_like(lse_scr)

    def hide(score):
        if not own:
            return score
        return jnp.concatenate([jnp.where(later, NEGATIVE, score[:, :128]), score[:, 128:]], axis=1)

    def pair_of_heads(step, carry):
        at = pl.multiple_of(step * 256, 256)
        rope_at = pl.multiple_of(HEADS * D_NOPE + step * 128, 128)
        nope = [jnp.concatenate([ref[i, run, pl.ds(at, 256)] for ref, i in q_refs], axis=0) for run in runs]
        ropes = [[ref[i, run, pl.ds(rope_at, 128)].astype(jnp.float32) for ref, i in q_refs] for run in runs]
        k_pair = [jnp.concatenate([ref[half, :, pl.ds(at, 256)] for ref in k_refs], axis=0) for half in range(2)]
        v_pair = [jnp.concatenate([ref[half, :, pl.ds(at, 256)] for ref in v_refs], axis=0) for half in range(2)]
        scores = []
        for inner in range(2):
            cols = slice(inner * 128, (inner + 1) * 128)

            def rows_of(half, fill):
                ends = [
                    jnp.where(lane < 64, pltpu.roll(r, 64, 1) if inner else r, f)
                    for r, f in zip(ropes[half], fill)
                ]
                ends = jnp.concatenate(ends, axis=0).astype(jnp.bfloat16)
                return jnp.concatenate([nope[half][:, cols], ends], axis=1)

            keys = [jnp.concatenate([k[:, cols], tail], axis=1) for k, tail in zip(k_pair, tails)]
            both = jnp.concatenate([rows_of(0, biases[0]), rows_of(1, [0.0] * len(q_refs))], axis=0)
            on_low = over_lanes(both, keys[0])
            on_high = over_lanes(rows_of(1, biases[1]), keys[1])
            scores.append((hide(on_low[:Q_TILE]), on_low[Q_TILE:], hide(on_high)))
        peaks = []
        for low, middle, high in scores:
            top = [jnp.max(s, axis=1, keepdims=True) for s in (low, middle, high)]
            peaks.append((jnp.maximum(top[0], FLOOR), jnp.maximum(top[1], jnp.maximum(top[2], FLOOR))))
        weights = []
        for (low, middle, high), (p_low, p_high) in zip(scores, peaks):
            on_low = [jnp.exp2(low - p_low).astype(jnp.bfloat16), jnp.exp2(middle - p_high).astype(jnp.bfloat16)]
            weights.append((jnp.concatenate(on_low, axis=0), jnp.exp2(high - p_high).astype(jnp.bfloat16)))
        sums = []
        for inner, (on_low, on_high) in enumerate(weights):
            cols = slice(inner * 128, (inner + 1) * 128)
            values = [jnp.concatenate([v[:, cols], ones], axis=1) for v in v_pair]
            a = jnp.dot(on_low, values[0], preferred_element_type=jnp.float32)
            b = jnp.dot(on_high, values[1], preferred_element_type=jnp.float32)
            sums.append((a[:Q_TILE], a[Q_TILE:] + b))
        for inner in range(2):
            head_at = pl.multiple_of(step * 256 + inner * 128, 128)
            for half in range(2):
                added, peak = sums[inner][half], peaks[inner][half]
                some = added[:, D_VAL:] > 0.0
                total = jnp.where(some, added[:, D_VAL:], 1.0)
                result = (added[:, :D_VAL] / total).astype(jnp.bfloat16)
                lse = jnp.where(some, peak + jnp.log2(total), NEGATIVE)
                for i in range(2 * X_SIZE):
                    rows = slice(i * RUN, (i + 1) * RUN)
                    outs[i // X_SIZE][i % X_SIZE, runs[half], pl.ds(head_at, 128)] = result[rows]
                    held = lse_scr[i, runs[half], :]
                    lse_scr[i, runs[half], :] = jnp.where(lane == 2 * step + inner, lse[rows], held)
        return carry

    lax.fori_loop(0, HEADS // 2, pair_of_heads, 0)
    for i in range(2 * X_SIZE):
        outs[i // X_SIZE][i % X_SIZE, :, HEADS * D_VAL :] = packed(lse_scr[i])


def attend(near, far, chunks, own):
    ks, vs, tails = zip(*chunks)
    out = jax.ShapeDtypeStruct((X_SIZE, TOK, OUT_ROW), jnp.bfloat16)
    return pl.pallas_call(
        functools.partial(attend_kernel, len(chunks), own),
        in_specs=[VMEM] * (2 + 3 * len(chunks)),
        out_specs=[VMEM] * 2,
        out_shape=[out, out],
        scratch_shapes=[pltpu.VMEM((2 * X_SIZE, TOK, 128), jnp.float32)],
        compiler_params=pltpu.CompilerParams(vmem_limit_bytes=22 << 20),
        cost_estimate=pl.CostEstimate(
            flops=10**7 * sum(a.shape[1] for a in ks), bytes_accessed=8 << 20, transcendentals=3 * 10**6
        ),
        name="attend",
    )(near, far, *ks, *vs, *tails)


def mix(parts, shares, run, h):
    cols = slice(h * D_VAL, (h + 1) * D_VAL)
    terms = [p[run, cols].astype(jnp.float32) * s[run, h : h + 1] for p, s in zip(parts, shares)]
    return functools.reduce(jnp.add, terms)


def merge_kernel(n_parts, which, *refs):
    for i, out_ref in zip(which, refs[n_parts:]):
        parts = [ref.at[i] for ref in refs[:n_parts]]
        stats = [unpacked(p[:, HEADS * D_VAL :]) for p in parts]
        best = functools.reduce(jnp.maximum, stats)
        shares = [jnp.exp2(s - best) for s in stats]
        whole = functools.reduce(jnp.add, shares)
        used = lanes(TOK) < HEADS
        out_ref[:, HEADS * D_VAL :] = packed(jnp.where(used, best + jnp.log2(whole), 0.0))
        shares = [s / whole for s in shares]
        for h in range(HEADS):
            out_ref[:, h * D_VAL : (h + 1) * D_VAL] = mix(parts, shares, slice(0, TOK), h).astype(jnp.bfloat16)


def merge(parts, which):
    return pl.pallas_call(
        functools.partial(merge_kernel, len(parts), which),
        in_specs=[VMEM] * len(parts),
        out_specs=[VMEM] * len(which),
        out_shape=[jax.ShapeDtypeStruct((TOK, OUT_ROW), jnp.bfloat16)] * len(which),
        compiler_params=pltpu.CompilerParams(vmem_limit_bytes=8 << 20),
        name="merge",
    )(*parts)


def combine_kernel(n_local, pos_ref, *refs):
    parts, out_ref = [ref.at[0] for ref in refs[:n_local]] + list(refs[n_local:-1]), refs[-1]
    stats = [unpacked(p[:, HEADS * D_VAL :]) for p in parts]
    best = functools.reduce(jnp.maximum, stats)
    shares = [jnp.exp2(s - best) for s in stats]
    whole = functools.reduce(jnp.add, shares)
    shares = [s / whole for s in shares]
    turn = jnp.where(pos_ref[0] < pos_ref[RUN], 0, RUN)
    for half in range(2):
        dst = pl.ds(pl.multiple_of(turn if half == 0 else RUN - turn, RUN), RUN)
        run = slice(half * RUN, (half + 1) * RUN)
        for h in range(HEADS):
            out_ref[dst, h * D_VAL : (h + 1) * D_VAL] = mix(parts, shares, run, h).astype(jnp.bfloat16)


def shift(size, by):
    return [(i, (i + by) % size) for i in range(size)]


def body(q_nope, q_rope, kv_compressed, token_pos, kv_gain, w_uk, w_uv):
    spans, steps = rotations()
    low_span = lambda i, pos: (jnp.minimum(pos[0], pos[RUN]) // RUN, 0, 0)
    high_span = lambda i, pos: (jnp.maximum(pos[0], pos[RUN]) // RUN, 0, 0)
    whole = lambda shape: pl.BlockSpec(shape, lambda i, pos: (0,) * len(shape))
    key_rows, q_rows = pl.pallas_call(
        rows_kernel,
        grid_spec=pltpu.PrefetchScalarGridSpec(
            num_scalar_prefetch=1,
            grid=(1,),
            in_specs=[
                pl.BlockSpec((1, 2, 128), low_span),
                pl.BlockSpec((1, 2, 128), high_span),
                whole((2, RUN, 128)),
                whole(q_nope.shape),
                whole(q_rope.shape),
                whole(kv_compressed.shape),
                whole((1, D_LAT)),
            ],
            out_specs=[whole((TOK, ROW)), whole((TOK, Q_ROW))],
        ),
        out_shape=[
            jax.ShapeDtypeStruct((TOK, ROW), jnp.bfloat16),
            jax.ShapeDtypeStruct((TOK, Q_ROW), jnp.bfloat16),
        ],
        name="rows",
    )(token_pos, spans, spans, steps, q_nope, q_rope, kv_compressed, kv_gain[None, :])

    swap = lambda block: lax.ppermute(block, "core", [(0, 1), (1, 0)])
    across = lambda block, by: lax.ppermute(block, ACROSS, shift(X_SIZE, by))
    along = lambda block, by: lax.ppermute(block, "z", shift(Z_SIZE, by))

    along_y = [lax.ppermute(key_rows, "y", shift(Y_SIZE, by)) for by in (1, -1, 2)]
    mine = jnp.stack([key_rows] + along_y)
    from_left = across(q_rows, 1)
    mine, q_rows, from_left = lax.optimization_barrier((mine, q_rows, from_left))

    up, down = along(mine, 1), along(mine, -1)
    opposite = across(q_rows, 2)
    first = [expand([mine], w_uk, w_uv)]
    up, down, opposite, q_rows, first = lax.optimization_barrier((up, down, opposite, q_rows, first))

    blocks = [up, down]
    up, down = along(up, 1), along(down, -1)
    from_right = across(q_rows, -1)
    first.append(expand(blocks, w_uk, w_uv))
    up, down, from_right, first = lax.optimization_barrier((up, down, from_right, first))

    blocks = [up, down]
    up, down = along(up, 1), along(down, -1)
    near = jnp.stack([q_rows, from_left, from_right, opposite])
    far = swap(near)
    second = [expand(blocks, w_uk, w_uv)]
    partials = [attend(near, far, first, True)]
    up, down, second, partials = lax.optimization_barrier((up, down, second, partials))

    half = Y_SIZE // 2
    blocks, ends = lax.optimization_barrier(([up, down], [up[:half], down[half:]]))
    up, down = along(ends[0], 1), along(ends[1], -1)
    second.append(expand(blocks, w_uk, w_uv))
    partials.append(attend(near, far, second, False))
    up, down, partials = lax.optimization_barrier((up, down, partials))

    crossed = [swap(p[1]) for p in partials]
    partials.append(attend(near, far, [expand([up, down], w_uk, w_uv)], False))
    crossed.append(swap(partials[2][1]))

    local = [p[0] for p in partials] + crossed
    opposite, = merge(local, [3])
    local, opposite = lax.optimization_barrier((local, opposite))
    right, left = merge(local, [1, 2])
    back = [across(m, by) for m, by in ((opposite, 2), (right, -1), (left, 1))]
    return pl.pallas_call(
        functools.partial(combine_kernel, len(local)),
        in_specs=[SMEM] + [VMEM] * (len(local) + 3),
        out_specs=VMEM,
        out_shape=jax.ShapeDtypeStruct((TOK, HEADS * D_VAL), jnp.bfloat16),
        compiler_params=pltpu.CompilerParams(vmem_limit_bytes=8 << 20),
        name="combine",
    )(token_pos, *local, *back)


def solution(mesh):
    finer = Mesh(mesh.devices.reshape(2, 2, Y_SIZE, Z_SIZE, 2), ALL_AXES)
    rows = P(ALL_AXES, None)
    in_specs = (rows, rows, rows, P(ALL_AXES), P(), P(), P())
    return jax.shard_map(body, mesh=finer, in_specs=in_specs, out_specs=rows, check_vma=False)
```
